512 devices in a mesh: bx: 16 (over z_hi, x, core), by: 32 (over z_lo, y).
Axes of the slice: x: 4, y: 8, z: 8 (z_hi: 2, z_lo: 4; z = z_hi * 4 + z_lo), core: 2. Of those that a mesh axis runs over, the one named last changes fastest.
Arguments:
- sources: bfloat16 [32, 16, 32, 1024], P(None, 'bx', 'by'), may hold values from -6 to 6
- near_blocks: bfloat16 [16, 32, 8, 9, 128, 128], P('bx', 'by'), may hold values from -0.1875 to 0.1875
- near_index: int32 [16, 32, 8, 9], P('bx', 'by'), may hold values from 0 to 7
- far_project: bfloat16 [16, 32, 1024, 128], P('bx', 'by'), may hold values from -0.1875 to 0.1875
- far_mixing: bfloat16 [16, 32, 9, 2, 128, 128], P('bx', 'by'), may hold values from -0.375 to 0.375
- far_expand: bfloat16 [16, 32, 128, 1024], P('bx', 'by'), may hold values from -0.5 to 0.5
Outputs:
- response: float32 [32, 16, 32, 1024], P(None, 'bx', 'by')
The draws below stay inside these ranges and needn't reach their ends.
Inputs may be any that keep to these rules, and one draw needn't show every extreme that they name: `near_index`: entry k of a block row's list names a block of the box at neighbour position k.
All inputs are finite; a program needn't handle non-finite values.
Results may differ from the reference program's by a relative error of at most 0.012.
Values may be sent and summed in bfloat16 or wider, within the bound.
No kernel may reach another device: no remote copies, remote signals or barrier semaphores. Data moves between devices by JAX's collectives and lax.ppermute only.
A program may use at most 64 MiB of HBM per device.

```python
import jax
import jax.numpy as jnp

RHS = 32
BLK_DEV = 8
BLOCK = 128
NEAR = 9
RANK = 128
UNK_DEV = 1024
BOXES_X = 16
BOXES_Y = 32
LEVELS_X = 4
LEVELS_Y = 5
LEVELS = 9


def set_ends(drawn, stream_key, least, high):
    dims = drawn.shape
    spot = [jax.random.randint(jax.random.fold_in(stream_key, axis), (), 0, dims[axis]) for axis in range(len(dims))]
    drawn = drawn.at[tuple(spot)].set(least)
    longest = dims.index(max(dims))
    spot[longest] = (spot[longest] + 1) % dims[longest]
    return drawn.at[tuple(spot)].set(high)


def steps_of(stream_key, shape, cuts, least, largest):
    factor_of, own = 1.0, jax.random.fold_in(stream_key, 6)
    for axis_at, parts in cuts:
        heights = jnp.exp(jax.random.uniform(jax.random.fold_in(own, axis_at), (parts,), jnp.float32, least / len(cuts), largest / len(cuts)))
        factor_of = factor_of * jnp.repeat(heights, shape[axis_at] // parts).reshape([-1 if axis == axis_at else 1 for axis in range(len(shape))])
    return factor_of


def centred(own_key, shape, deviation, reach, pieces=(), held_as=jnp.bfloat16):
    array = jax.random.normal(own_key, shape, jnp.float32) * deviation
    if len(pieces) > 0:
        array = steps_of(own_key, shape, pieces, -0.22, 0.18) * array
    return jnp.clip(array, min=-reach, max=reach).astype(held_as)


def setup_inputs(seed: int = 0) -> dict:
    key_list = jax.random.split(jax.random.key(seed), 7)
    sources = centred(key_list[0], (RHS, BOXES_X, BOXES_Y, UNK_DEV), 1.0, 6.0, ((1, 16), (2, 32)))
    near_blocks = centred(key_list[1], (BOXES_X, BOXES_Y, BLK_DEV, NEAR, BLOCK, BLOCK), (NEAR * BLOCK) ** -0.5, 0.1875, ((0, 16), (1, 32)))
    near_index = set_ends(jax.random.randint(key_list[2], (BOXES_X, BOXES_Y, BLK_DEV, NEAR), 0, BLK_DEV), jax.random.fold_in(key_list[2], 1), 0, BLK_DEV - 1).astype(jnp.int32)
    far_project = centred(key_list[3], (BOXES_X, BOXES_Y, UNK_DEV, RANK), UNK_DEV ** -0.5, 0.1875, ((0, 16), (1, 32)))
    far_mixing = centred(key_list[4], (BOXES_X, BOXES_Y, LEVELS, 2, RANK, RANK), (2 * RANK) ** -0.5, 0.375, ((0, 16), (1, 32)))
    far_expand = centred(key_list[5], (BOXES_X, BOXES_Y, RANK, UNK_DEV), RANK ** -0.5, 0.5, ((0, 16), (1, 32)))
    return dict(sources=sources, near_blocks=near_blocks, near_index=near_index, far_project=far_project, far_mixing=far_mixing, far_expand=far_expand)


def flip_pairs(values, axis_dim, stride):
    old_shape = values.shape
    count_boxes = old_shape[axis_dim]
    new_shape = old_shape[:axis_dim] + (count_boxes // (2 * stride), 2, stride) + old_shape[axis_dim + 1:]
    return jnp.flip(values.reshape(new_shape), axis_dim + 1).reshape(old_shape)


def mix_level(coeffs, partner, mixing):
    own_term = jnp.einsum('cxyr,xyrq->cxyq', coeffs.astype(jnp.float32), mixing[:, :, 0].astype(jnp.float32))
    other_term = jnp.einsum('cxyr,xyrq->cxyq', partner.astype(jnp.float32), mixing[:, :, 1].astype(jnp.float32))
    return (own_term + other_term).astype(jnp.bfloat16)


def reference(sources, near_blocks, near_index, far_project, far_mixing, far_expand):
    padded = jnp.pad(sources, ((0, 0), (1, 1), (1, 1), (0, 0)))
    accum_near = jnp.zeros((RHS, BOXES_X, BOXES_Y, BLK_DEV, BLOCK), jnp.float32)
    for neighbour in range(NEAR):
        shift_x = neighbour // 3
        shift_y = neighbour % 3
        window = padded[:, shift_x:shift_x + BOXES_X, shift_y:shift_y + BOXES_Y, :]
        window = window.reshape(RHS, BOXES_X, BOXES_Y, BLK_DEV, BLOCK)
        which_block = near_index[:, :, :, neighbour].astype(jnp.int32)
        chosen = jnp.take_along_axis(window, which_block[None, :, :, :, None], axis=3)
        accum_near = accum_near + jnp.einsum('xyrij,cxyrj->cxyri', near_blocks[:, :, :, neighbour].astype(jnp.float32), chosen.astype(jnp.float32))
    near_part = accum_near.reshape(RHS, BOXES_X, BOXES_Y, UNK_DEV)
    coeffs = jnp.einsum('cxyu,xyur->cxyr', sources.astype(jnp.float32), far_project.astype(jnp.float32)).astype(jnp.bfloat16)
    for level_num in range(LEVELS_X):
        partner = flip_pairs(coeffs, 1, 2 ** level_num)
        coeffs = mix_level(coeffs, partner, far_mixing[:, :, level_num])
    for level_num in range(LEVELS_Y):
        partner = flip_pairs(coeffs, 2, 2 ** level_num)
        coeffs = mix_level(coeffs, partner, far_mixing[:, :, LEVELS_X + level_num])
    far_part = jnp.einsum('cxyr,xyru->cxyu', coeffs.astype(jnp.float32), far_expand.astype(jnp.float32))
    return near_part + far_part
```

```python
import jax
import jax.numpy as jnp
from jax import lax
from jax.sharding import PartitionSpec as P


def with_halo(block, sides, width):
    for axis, dim in sides:
        count = lax.axis_size(axis)
        forward = [(i, i + 1) for i in range(count - 1)]
        backward = [(target, source) for source, target in forward]
        low = lax.ppermute(
            lax.slice_in_dim(block, block.shape[dim] - width, None, axis=dim), axis, forward
        )
        high = lax.ppermute(lax.slice_in_dim(block, 0, width, axis=dim), axis, backward)
        block = jnp.concatenate([low, block, high], axis=dim)
    return block


def near_field(sources, near_blocks, near_index):
    excite = sources.shape[0]
    blocks = near_blocks.shape[2]
    positions = near_blocks.shape[3]
    block_len = near_blocks.shape[4]
    beside_all = with_halo(sources, (("bx", 1), ("by", 2)), 1)
    source_blocks = beside_all.reshape(excite, positions, blocks, block_len)
    onehot = (
        near_index[0, 0][:, :, None] == jnp.arange(blocks, dtype=jnp.int32)[None, None, :]
    ).astype(jnp.bfloat16)
    picked = jnp.einsum(
        "rkb,ckbj->rkcj", onehot, source_blocks, preferred_element_type=jnp.float32
    ).astype(jnp.bfloat16)
    near_sum = jnp.einsum(
        "rkij,rkcj->cri", near_blocks[0, 0], picked, preferred_element_type=jnp.float32
    )
    return near_sum.reshape(excite, 1, 1, blocks * block_len)


def pair_gather(coeffs, axis, apart):
    count = lax.axis_size(axis)
    pairs = [[i, i ^ 1 << apart] for i in range(count) if not i >> apart & 1]
    return lax.all_gather(coeffs, axis, axis_index_groups=pairs)


def far_field(sources, far_project, far_mixing, far_expand):
    excite = sources.shape[0]
    unknowns = sources.shape[3]
    levels = [("bx", n) for n in range(lax.axis_size("bx").bit_length() - 1)]
    levels += [("by", n) for n in range(lax.axis_size("by").bit_length() - 1)]
    upper = jnp.stack([lax.axis_index(axis) >> n & 1 for axis, n in levels])
    mixing = far_mixing[0, 0]
    mixing = lax.optimization_barrier(
        jnp.where(upper[:, None, None, None] == 1, mixing[:, ::-1], mixing)
    )
    coeffs = jnp.dot(
        sources[:, 0, 0], far_project[0, 0], preferred_element_type=jnp.float32
    ).astype(jnp.bfloat16)
    for level_num, (axis, apart) in enumerate(levels):
        both = pair_gather(coeffs, axis, apart)
        coeffs = jnp.einsum(
            "bcr,brq->cq", both, mixing[level_num], preferred_element_type=jnp.float32
        ).astype(jnp.bfloat16)
    far_sum = jnp.dot(coeffs, far_expand[0, 0], preferred_element_type=jnp.float32)
    return far_sum.reshape(excite, 1, 1, unknowns)


def per_device(sources, near_blocks, near_index, far_project, far_mixing, far_expand):
    near_part = near_field(sources, near_blocks, near_index)
    far_part = far_field(sources, far_project, far_mixing, far_expand)
    return near_part + far_part


def solution(mesh):
    placed = (
        P(None, "bx", "by", None),
        P("bx", "by", None, None, None, None),
        P("bx", "by", None, None),
        P("bx", "by", None, None),
        P("bx", "by", None, None, None, None),
        P("bx", "by", None, None),
    )
    return jax.shard_map(
        per_device, mesh=mesh, in_specs=placed, out_specs=P(None, "bx", "by", None), check_vma=False
    )
```

```python
import functools

import jax
import jax.numpy as jnp
from jax import lax
from jax.experimental import pallas as pl
from jax.experimental.pallas import tpu as pltpu
from jax.sharding import PartitionSpec as P

BOTH = ("bx", "by")


def pair_gather(values, axis, apart):
    count = lax.axis_size(axis)
    pairs = [[i, i ^ 1 << apart] for i in range(count) if not i >> apart & 1]
    return lax.all_gather(values, axis, axis_index_groups=pairs)


def handed(values, source):
    pairs = [(i, i ^ 1) for i in range(lax.axis_size("bx")) if i & 1 == source]
    return lax.ppermute(values, "bx", pairs)


def sent_on(values, step_x, step_y):
    count_x, count_y = lax.axis_size("bx"), lax.axis_size("by")
    moves = []
    for x in range(0, count_x, 2):
        for y in range(count_y):
            to_x, to_y = x + step_x, y + step_y
            if 0 <= to_x < count_x and 0 <= to_y < count_y:
                moves.append((x * count_y + y, to_x * count_y + to_y))
    return lax.ppermute(values, BOTH, moves)


def surroundings(sources):
    below, above = sent_on(sources, 0, 1), sent_on(sources, 0, -1)
    column = jnp.stack([below, sources, above], axis=1)
    before, after = sent_on(column[1], 2, 0), sent_on(column[0], -2, 0)
    return jnp.concatenate([before[None], column, after[None]])


def near_field(around, near_blocks, near_index):
    positions, excite, unknowns = around.shape
    blocks, block_len = near_blocks.shape[0], near_blocks.shape[2]
    source_blocks = around.reshape(positions, excite, blocks, block_len)
    onehot = (
        near_index[:, :, None] == jnp.arange(blocks, dtype=near_index.dtype)[None, None, :]
    ).astype(jnp.bfloat16)
    picked = jnp.einsum(
        "rkb,kcbj->rkcj", onehot, source_blocks, preferred_element_type=jnp.float32
    ).astype(jnp.bfloat16)
    near_sum = jnp.einsum(
        "rkij,rkcj->cri", near_blocks, picked, preferred_element_type=jnp.float32
    )
    return near_sum.reshape(excite, unknowns)


def order_levels(levels, theirs_hbm, own_hbm, ordered, sems):
    copies = []
    for box, blocks in enumerate((theirs_hbm, own_hbm)):
        for at, (axis, apart) in enumerate(levels):
            upper = lax.axis_index(axis) >> apart & 1
            for member in range(2):
                copy = pltpu.make_async_copy(
                    blocks.at[at + 1, member ^ upper],
                    ordered.at[box, at, member],
                    sems.at[box, at, member],
                )
                copy.start()
                copies.append(copy)
    for copy in copies:
        copy.wait()


def butterfly(coeffs, theirs, own):
    levels = [("bx", n) for n in range(1, lax.axis_size("bx").bit_length() - 1)]
    levels += [("by", n) for n in range(lax.axis_size("by").bit_length() - 1)]
    count, rank = len(levels), own.shape[-1]
    ordered = pl.pallas_call(
        functools.partial(order_levels, levels),
        out_shape=jax.ShapeDtypeStruct((2, count, 2, rank, rank), own.dtype),
        in_specs=[pl.BlockSpec(memory_space=pl.ANY)] * 2,
        out_specs=pl.BlockSpec(memory_space=pltpu.VMEM),
        scratch_shapes=[pltpu.SemaphoreType.DMA((2, count, 2))],
    )(theirs, own)
    first = jnp.stack([theirs[0], own[0][::-1]])
    coeffs = jnp.einsum(
        "gcr,bgrq->bcq", coeffs, first, preferred_element_type=jnp.float32
    ).astype(jnp.bfloat16)
    for at, (axis, apart) in enumerate(levels):
        both = pair_gather(coeffs, axis, apart)
        coeffs = jnp.einsum(
            "gbcr,bgrq->bcq", both, ordered[:, at], preferred_element_type=jnp.float32
        ).astype(jnp.bfloat16)
    return coeffs


def per_device(sources, near_blocks, near_index, far_project, far_mixing, far_expand):
    own_sources, own_blocks, own_index = sources[:, 0, 0], near_blocks[0, 0], near_index[0, 0]
    own_mixing = far_mixing[0, 0]
    excite, unknowns = own_sources.shape
    rank = far_project.shape[3]
    core = lax.axis_index("bx") & 1
    their_mixing = handed(own_mixing, 0)
    their_blocks = handed(own_blocks, 1)
    coeffs = jnp.dot(
        own_sources, far_project[0, 0], preferred_element_type=jnp.float32
    ).astype(jnp.bfloat16)
    rows, positions = own_index.shape
    index_values = jnp.pad(
        own_index.astype(jnp.bfloat16), ((0, excite - rows), (0, 128 - positions))
    )
    shared = pair_gather(
        jnp.concatenate([own_sources, coeffs, index_values], axis=1), "bx", 0
    )

    def near_fields():
        around = surroundings(shared[:, :, :unknowns])
        their_index = shared[1, :rows, unknowns + rank : unknowns + rank + positions]
        mine = near_field(
            around[:3].reshape(-1, excite, unknowns), own_blocks, own_index
        )
        theirs = near_field(
            around[1:].reshape(-1, excite, unknowns), their_blocks, their_index.astype(jnp.int32)
        )
        return mine, theirs, jnp.zeros((excite, rank), jnp.bfloat16)

    def butterflies():
        final = butterfly(shared[:, :, unknowns : unknowns + rank], their_mixing, own_mixing)
        given = jnp.pad(final[0].astype(jnp.float32), ((0, 0), (0, unknowns - rank)))
        return given, given, final[1]

    mine, given, final = lax.cond(core == 0, near_fields, butterflies)
    taken = pair_gather(given, "bx", 0)
    near_part = jnp.where(core == 0, mine, taken[0])
    final = jnp.where(core == 0, taken[1, :, :rank].astype(jnp.bfloat16), final)
    far_part = jnp.dot(final, far_expand[0, 0], preferred_element_type=jnp.float32)
    return (near_part + far_part)[:, None, None]


def solution(mesh):
    placed = (
        P(None, "bx", "by", None),
        P("bx", "by", None, None, None, None),
        P("bx", "by", None, None),
        P("bx", "by", None, None),
        P("bx", "by", None, None, None, None),
        P("bx", "by", None, None),
    )
    return jax.shard_map(
        per_device, mesh=mesh, in_specs=placed, out_specs=P(None, "bx", "by", None), check_vma=False
    )
```

```python
import functools

import jax
import jax.numpy as jnp
from jax import lax
from jax.experimental import pallas as pl
from jax.experimental.pallas import tpu as pltpu
from jax.sharding import PartitionSpec as P

BOTH = ("bx", "by")
LANES = 128


def pair_gather(values, axis, apart):
    count = lax.axis_size(axis)
    pairs = [[i, i ^ 1 << apart] for i in range(count) if not i >> apart & 1]
    return lax.all_gather(values, axis, axis_index_groups=pairs)


def sent_on(values, step_x, step_y):
    count_x, count_y = lax.axis_size("bx"), lax.axis_size("by")
    moves = []
    for x in range(0, count_x, 2):
        for y in range(count_y):
            to_x, to_y = x + step_x, y + step_y
            if 0 <= to_x < count_x and 0 <= to_y < count_y:
                moves.append((x * count_y + y, to_x * count_y + to_y))
    return lax.ppermute(values, BOTH, moves)


def surroundings(sources):
    below, above = sent_on(sources, 0, 1), sent_on(sources, 0, -1)
    column = jnp.stack([below, sources, above], axis=1)
    before, after = sent_on(column[1], 2, 0), sent_on(column[0], -2, 0)
    return jnp.concatenate([before[None], column, after[None]])


def near_field(around, near_blocks, near_index):
    positions, excite, unknowns = around.shape
    blocks, block_len = near_blocks.shape[0], near_blocks.shape[2]
    source_blocks = around.reshape(positions, excite, blocks, block_len)
    onehot = (
        near_index[:, :, None] == jnp.arange(blocks, dtype=near_index.dtype)[None, None, :]
    ).astype(jnp.bfloat16)
    picked = jnp.einsum(
        "rkb,kcbj->rkcj", onehot, source_blocks, preferred_element_type=jnp.float32
    ).astype(jnp.bfloat16)
    near_sum = jnp.einsum(
        "rkij,rkcj->cri", near_blocks, picked, preferred_element_type=jnp.float32
    )
    return near_sum.reshape(excite, unknowns)


class Packing:
    def __init__(self, mixing_rows, excite, unknowns):
        self.excite, self.blocks = excite, unknowns // LANES
        self.coeffs = mixing_rows
        self.sources = self.coeffs + excite
        self.index = self.sources + self.blocks * excite
        self.rows = self.index + excite


def pack(packing, mixing_hbm, sources_hbm, project_hbm, index_ref, packed, sources, project, sems):
    excite = packing.excite
    wide = [
        pltpu.make_async_copy(sources_hbm, sources, sems.at[0]),
        pltpu.make_async_copy(project_hbm, project, sems.at[1]),
    ]
    for copy in wide:
        copy.start()
    rest = [
        pltpu.make_async_copy(mixing_hbm, packed.at[pl.ds(0, packing.coeffs)], sems.at[2])
    ]
    for block in range(packing.blocks):
        rest.append(
            pltpu.make_async_copy(
                sources_hbm.at[:, pl.ds(block * LANES, LANES)],
                packed.at[pl.ds(packing.sources + block * excite, excite)],
                sems.at[3 + block],
            )
        )
    for copy in rest:
        copy.start()
    rows, positions = index_ref.shape
    index = jnp.concatenate(
        [index_ref[...], jnp.zeros((rows, LANES - positions), jnp.int32)], axis=1
    )
    index = jnp.concatenate([index, jnp.zeros((excite - rows, LANES), jnp.int32)], axis=0)
    packed[pl.ds(packing.index, excite)] = index.astype(jnp.float32).astype(jnp.bfloat16)
    for copy in wide:
        copy.wait()
    packed[pl.ds(packing.coeffs, excite)] = jnp.dot(
        sources[...], project[...], preferred_element_type=jnp.float32
    ).astype(jnp.bfloat16)
    for copy in rest:
        copy.wait()


def packed_own(packing, mixing, sources, project, index):
    rank = project.shape[1]
    return pl.pallas_call(
        functools.partial(pack, packing),
        name="pack",
        out_shape=pltpu.VMEM((packing.rows, LANES), jnp.bfloat16),
        in_specs=[pl.BlockSpec(memory_space=pl.ANY)] * 3
        + [pl.BlockSpec(memory_space=pltpu.VMEM)],
        out_specs=pl.BlockSpec(memory_space=pltpu.VMEM),
        scratch_shapes=[
            pltpu.VMEM(sources.shape, sources.dtype),
            pltpu.VMEM(project.shape, project.dtype),
            pltpu.SemaphoreType.DMA((3 + packing.blocks,)),
        ],
    )(mixing.reshape(-1, rank), sources, project, index)


def first_level(packing, theirs, own, coeffs):
    excite, rank = packing.excite, coeffs.shape[2]
    given = [ref[pl.ds(packing.coeffs, excite)] for ref in (theirs, own)]
    for box, ref in enumerate((theirs, own)):
        pair = jnp.concatenate([given[box], given[1 - box]], axis=1)
        coeffs[box] = jnp.dot(
            pair, ref[pl.ds(0, 2 * rank)], preferred_element_type=jnp.float32
        ).astype(coeffs.dtype)


def mixed(packing, level, place, both, theirs, own):
    axis, apart = place
    rank = both.shape[3]
    upper = lax.axis_index(axis) >> apart & 1
    sums = []
    for box, ref in enumerate((theirs, own)):
        pair = jnp.concatenate([both[upper, box], both[1 - upper, box]], axis=1)
        sums.append(
            jnp.dot(
                pair, ref[pl.ds(level * 2 * rank, 2 * rank)], preferred_element_type=jnp.float32
            ).astype(jnp.bfloat16)
        )
    return sums


def next_level(packing, level, place, both, theirs, own, coeffs):
    for box, value in enumerate(mixed(packing, level, place, both, theirs, own)):
        coeffs[box] = value


def last_level(packing, level, place, both, theirs, own, given, final):
    value, final[...] = mixed(packing, level, place, both, theirs, own)
    rank = value.shape[1]
    given[:, rank:] = jnp.zeros((given.shape[0], given.shape[1] - rank), given.dtype)
    given[:, :rank] = value.astype(given.dtype)


def in_vmem(kernel, name, out_shape, operands):
    return pl.pallas_call(
        kernel,
        name=name,
        out_shape=out_shape,
        in_specs=[pl.BlockSpec(memory_space=pltpu.VMEM)] * operands,
        out_specs=jax.tree.map(lambda _: pl.BlockSpec(memory_space=pltpu.VMEM), out_shape),
    )


def butterfly(packing, theirs, own, rank, unknowns):
    excite = packing.excite
    levels = [("bx", n) for n in range(lax.axis_size("bx").bit_length() - 1)]
    levels += [("by", n) for n in range(lax.axis_size("by").bit_length() - 1)]
    shape = pltpu.VMEM((2, excite, rank), jnp.bfloat16)
    coeffs = in_vmem(functools.partial(first_level, packing), "level_0", shape, 2)(theirs, own)
    for level, place in enumerate(levels):
        if level == 0:
            continue
        both = pair_gather(coeffs, *place)
        kernel = functools.partial(next_level, packing, level, place)
        if level == len(levels) - 1:
            kernel = functools.partial(last_level, packing, level, place)
            shape = (
                pltpu.VMEM((excite, unknowns), jnp.float32),
                pltpu.VMEM((excite, rank), jnp.bfloat16),
            )
        coeffs = in_vmem(kernel, f"level_{level}", shape, 3)(both, theirs, own)
    return coeffs


def per_device(sources, near_blocks, near_index, far_project, far_mixing, far_expand):
    own_sources, own_blocks, own_index = sources[:, 0, 0], near_blocks[0, 0], near_index[0, 0]
    excite, unknowns = own_sources.shape
    rank = far_project.shape[3]
    rows, positions = own_index.shape
    core = lax.axis_index("bx") & 1
    packing = Packing(far_mixing[0, 0].size // rank, excite, unknowns)
    packed = packed_own(packing, far_mixing[0, 0], own_sources, far_project[0, 0], own_index)
    partners = [(i, i ^ 1) for i in range(lax.axis_size("bx"))]
    theirs = lax.ppermute(packed, "bx", partners)
    their_blocks = lax.ppermute(own_blocks, "bx", partners[1::2])

    def near_fields():
        their_sources = theirs[packing.sources : packing.index]
        their_sources = their_sources.reshape(packing.blocks, excite, LANES)
        their_sources = their_sources.transpose(1, 0, 2).reshape(excite, unknowns)
        around = surroundings(jnp.stack([own_sources, their_sources]))
        their_index = theirs[packing.index : packing.index + rows, :positions].astype(jnp.int32)
        mine = near_field(around[:3].reshape(-1, excite, unknowns), own_blocks, own_index)
        given = near_field(around[1:].reshape(-1, excite, unknowns), their_blocks, their_index)
        return mine, given, jnp.zeros((excite, rank), jnp.bfloat16)

    def butterflies():
        given, final = butterfly(packing, theirs, packed, rank, unknowns)
        return given, given, final

    mine, given, final = lax.cond(core == 0, near_fields, butterflies)
    taken = pair_gather(given, "bx", 0)
    near_part = jnp.where(core == 0, mine, taken[0])
    final = jnp.where(core == 0, taken[1, :, :rank].astype(jnp.bfloat16), final)
    far_part = jnp.dot(final, far_expand[0, 0], preferred_element_type=jnp.float32)
    return (near_part + far_part)[:, None, None]


def solution(mesh):
    placed = (
        P(None, "bx", "by", None),
        P("bx", "by", None, None, None, None),
        P("bx", "by", None, None),
        P("bx", "by", None, None),
        P("bx", "by", None, None, None, None),
        P("bx", "by", None, None),
    )
    return jax.shard_map(
        per_device, mesh=mesh, in_specs=placed, out_specs=P(None, "bx", "by", None), check_vma=False
    )
```

```python
import functools

import jax
import jax.numpy as jnp
from jax import lax
from jax.experimental import pallas as pl
from jax.experimental.pallas import tpu as pltpu
from jax.sharding import PartitionSpec as P

BOTH = ("bx", "by")
LANES = 128


def pair_gather(values, axis, apart):
    count = lax.axis_size(axis)
    pairs = [[i, i ^ 1 << apart] for i in range(count) if not i >> apart & 1]
    return lax.all_gather(values, axis, axis_index_groups=pairs)


def sent_on(values, step_x, step_y):
    count_x, count_y = lax.axis_size("bx"), lax.axis_size("by")
    moves = []
    for x in range(0, count_x, 2):
        for y in range(count_y):
            to_x, to_y = x + step_x, y + step_y
            if 0 <= to_x < count_x and 0 <= to_y < count_y:
                moves.append((x * count_y + y, to_x * count_y + to_y))
    return lax.ppermute(values, BOTH, moves)


def surroundings(sources):
    before, after = sent_on(sources[1], 2, 0), sent_on(sources[0], -2, 0)
    row = jnp.concatenate([before[None], sources, after[None]])
    return jnp.stack([sent_on(row, 0, 1), row, sent_on(row, 0, -1)], axis=1)


def near_field(around, near_blocks, near_index):
    blocks, excite, lanes = around.shape[2:]
    source_blocks = around.reshape(-1, blocks, excite, lanes)
    onehot = (
        near_index[:, :, None] == jnp.arange(blocks, dtype=near_index.dtype)[None, None, :]
    ).astype(jnp.bfloat16)
    picked = jnp.einsum(
        "rkb,kbcj->rkcj", onehot, source_blocks, preferred_element_type=jnp.float32
    ).astype(jnp.bfloat16)
    near_sum = jnp.einsum(
        "rkij,rkcj->cri", near_blocks, picked, preferred_element_type=jnp.float32
    )
    return near_sum.reshape(excite, blocks * lanes)


class Packing:
    def __init__(self, levels, rank, excite, unknowns):
        self.excite, self.blocks = excite, unknowns // LANES
        self.split = levels // 2
        self.level_rows = 2 * rank
        self.coeffs = self.split * self.level_rows
        self.sources = self.coeffs + excite
        self.index = self.sources + self.blocks * excite
        self.rows = (self.index + excite, (levels - self.split) * self.level_rows)

    def of_level(self, level):
        late = level >= self.split
        return int(late), pl.ds((level - self.split * late) * self.level_rows, self.level_rows)


def pack(
    packing, mixing_hbm, sources_hbm, project_hbm, index_ref, packed, later, sources, project, sems
):
    excite = packing.excite
    wide = [
        pltpu.make_async_copy(sources_hbm, sources, sems.at[0]),
        pltpu.make_async_copy(project_hbm, project, sems.at[1]),
    ]
    for copy in wide:
        copy.start()
    rest = [
        pltpu.make_async_copy(
            mixing_hbm.at[pl.ds(0, packing.coeffs)],
            packed.at[pl.ds(0, packing.coeffs)],
            sems.at[2],
        ),
        pltpu.make_async_copy(
            mixing_hbm.at[pl.ds(packing.coeffs, packing.rows[1])], later, sems.at[3]
        ),
    ]
    for block in range(packing.blocks):
        rest.append(
            pltpu.make_async_copy(
                sources_hbm.at[:, pl.ds(block * LANES, LANES)],
                packed.at[pl.ds(packing.sources + block * excite, excite)],
                sems.at[4 + block],
            )
        )
    for copy in rest:
        copy.start()
    rows, positions = index_ref.shape
    index = jnp.concatenate(
        [index_ref[...], jnp.zeros((rows, LANES - positions), jnp.int32)], axis=1
    )
    index = jnp.concatenate([index, jnp.zeros((excite - rows, LANES), jnp.int32)], axis=0)
    packed[pl.ds(packing.index, excite)] = index.astype(jnp.float32).astype(jnp.bfloat16)
    for copy in wide:
        copy.wait()
    packed[pl.ds(packing.coeffs, excite)] = jnp.dot(
        sources[...], project[...], preferred_element_type=jnp.float32
    ).astype(jnp.bfloat16)
    for copy in rest:
        copy.wait()


def packed_own(packing, mixing, sources, project, index):
    vmem = pl.BlockSpec(memory_space=pltpu.VMEM)
    return pl.pallas_call(
        functools.partial(pack, packing),
        name="pack",
        out_shape=tuple(pltpu.VMEM((rows, LANES), jnp.bfloat16) for rows in packing.rows),
        in_specs=[pl.BlockSpec(memory_space=pl.ANY)] * 3 + [vmem],
        out_specs=(vmem, vmem),
        scratch_shapes=[
            pltpu.VMEM(sources.shape, sources.dtype),
            pltpu.VMEM(project.shape, project.dtype),
            pltpu.SemaphoreType.DMA((4 + packing.blocks,)),
        ],
    )(mixing.reshape(-1, LANES), sources, project, index)


def first_level(packing, early, coeffs):
    given = [early[box, pl.ds(packing.coeffs, packing.excite)] for box in range(2)]
    rows = packing.of_level(0)[1]
    for box in range(2):
        pair = jnp.concatenate([given[box], given[1 - box]], axis=1)
        coeffs[box] = jnp.dot(
            pair, early[box, rows], preferred_element_type=jnp.float32
        ).astype(coeffs.dtype)


def mixed(packing, level, place, both, blocks):
    axis, apart = place
    upper = lax.axis_index(axis) >> apart & 1
    rows = packing.of_level(level)[1]
    sums = []
    for box in range(2):
        pair = jnp.concatenate([both[upper, box], both[1 - upper, box]], axis=1)
        sums.append(
            jnp.dot(pair, blocks[box, rows], preferred_element_type=jnp.float32).astype(
                jnp.bfloat16
            )
        )
    return sums


def next_level(packing, level, place, both, blocks, coeffs):
    for box, value in enumerate(mixed(packing, level, place, both, blocks)):
        coeffs[box] = value


def last_level(packing, level, place, both, blocks, given, final):
    value, final[...] = mixed(packing, level, place, both, blocks)
    rank = value.shape[1]
    given[:, rank:] = jnp.zeros((given.shape[0], given.shape[1] - rank), given.dtype)
    given[:, :rank] = value.astype(given.dtype)


def in_vmem(kernel, name, out_shape, operands):
    vmem = pl.BlockSpec(memory_space=pltpu.VMEM)
    call = pl.pallas_call(
        kernel,
        name=name,
        out_shape=out_shape,
        in_specs=[vmem] * len(operands),
        out_specs=jax.tree.map(lambda _: vmem, out_shape),
    )
    return call(*(pltpu.with_memory_space_constraint(x, pltpu.VMEM) for x in operands))


def butterfly_levels(packing, shared, levels, coeffs, first, last, unknowns):
    excite, rank = packing.excite, LANES
    for level in range(first, last):
        if level == 0:
            shape = pltpu.VMEM((2, excite, rank), jnp.bfloat16)
            kernel = functools.partial(first_level, packing)
            coeffs = in_vmem(kernel, "level_0", shape, (shared[0],))
            continue
        place = levels[level]
        both = pair_gather(coeffs, *place)
        kernel = functools.partial(next_level, packing, level, place)
        shape = pltpu.VMEM((2, excite, rank), jnp.bfloat16)
        if level == len(levels) - 1:
            kernel = functools.partial(last_level, packing, level, place)
            shape = (
                pltpu.VMEM((excite, unknowns), jnp.float32),
                pltpu.VMEM((excite, rank), jnp.bfloat16),
            )
        blocks = shared[packing.of_level(level)[0]]
        coeffs = in_vmem(kernel, f"level_{level}", shape, (both, blocks))
    return coeffs


def per_device(sources, near_blocks, near_index, far_project, far_mixing, far_expand):
    own_sources, own_blocks, own_index = sources[:, 0, 0], near_blocks[0, 0], near_index[0, 0]
    excite, unknowns = own_sources.shape
    rank = far_project.shape[3]
    rows, positions = own_index.shape
    first_of_pair = lax.axis_index("bx") & 1 == 0
    levels = [("bx", n) for n in range(lax.axis_size("bx").bit_length() - 1)]
    levels += [("by", n) for n in range(lax.axis_size("by").bit_length() - 1)]
    packing = Packing(len(levels), rank, excite, unknowns)
    packed = packed_own(packing, far_mixing[0, 0], own_sources, far_project[0, 0], own_index)
    shared = tuple(pair_gather(array, "bx", 0) for array in packed)
    butterfly = functools.partial(butterfly_levels, packing, shared, levels, unknowns=unknowns)
    late = len(levels) - 3

    def gathering():
        boxes = shared[0][:, packing.sources : packing.index]
        around = surroundings(boxes.reshape(2, packing.blocks, excite, LANES))
        return around, jnp.zeros((2, excite, rank), jnp.bfloat16)

    def levels_early():
        around = jnp.zeros((4, 3, packing.blocks, excite, LANES), jnp.bfloat16)
        return around, butterfly(None, 0, late)

    around, coeffs = lax.cond(first_of_pair, gathering, levels_early)
    handed_blocks, coeffs = lax.optimization_barrier((own_blocks, coeffs))
    handed = [(i, i ^ 1) for i in range(1, lax.axis_size("bx"), 2)]
    their_blocks = lax.ppermute(handed_blocks, "bx", handed)

    def near_own():
        return near_field(around[:3], own_blocks, own_index), coeffs

    def level_between():
        return jnp.zeros((excite, unknowns), jnp.float32), butterfly(coeffs, late, late + 1)

    mine, coeffs = lax.cond(first_of_pair, near_own, level_between)

    def near_other():
        index = shared[0][1, packing.index : packing.index + rows, :positions].astype(jnp.int32)
        return near_field(around[1:], their_blocks, index), jnp.zeros((excite, rank), jnp.bfloat16)

    def levels_late():
        return tuple(butterfly(coeffs, late + 1, len(levels)))

    given, final = lax.cond(first_of_pair, near_other, levels_late)
    taken = pair_gather(given, "bx", 0)
    near_part = jnp.where(first_of_pair, mine, taken[0])
    final = jnp.where(first_of_pair, taken[1, :, :rank].astype(jnp.bfloat16), final)
    far_part = jnp.dot(final, far_expand[0, 0], preferred_element_type=jnp.float32)
    return (near_part + far_part)[:, None, None]


def solution(mesh):
    placed = (
        P(None, "bx", "by", None),
        P("bx", "by", None, None, None, None),
        P("bx", "by", None, None),
        P("bx", "by", None, None),
        P("bx", "by", None, None, None, None),
        P("bx", "by", None, None),
    )
    return jax.shard_map(
        per_device, mesh=mesh, in_specs=placed, out_specs=P(None, "bx", "by", None), check_vma=False
    )
```

```python
import functools

import jax
import jax.numpy as jnp
from jax import lax
from jax.experimental import pallas as pl
from jax.experimental.pallas import tpu as pltpu
from jax.sharding import PartitionSpec as P

BOTH = ("bx", "by")
LANES = 128


def pair_gather(values, axis, apart):
    count = lax.axis_size(axis)
    pairs = [[i, i ^ 1 << apart] for i in range(count) if not i >> apart & 1]
    return lax.all_gather(values, axis, axis_index_groups=pairs)


def sent_on(values, step_x, step_y):
    count_x, count_y = lax.axis_size("bx"), lax.axis_size("by")
    moves = []
    for x in range(0, count_x, 2):
        for y in range(count_y):
            to_x, to_y = x + step_x, y + step_y
            if 0 <= to_x < count_x and 0 <= to_y < count_y:
                moves.append((x * count_y + y, to_x * count_y + to_y))
    return lax.ppermute(values, BOTH, moves)


class Packing:
    def __init__(self, levels, rank, excite, unknowns):
        self.excite, self.blocks = excite, unknowns // LANES
        self.split = levels // 2
        self.level_rows = 2 * rank
        self.box_rows = self.blocks * excite
        self.coeffs = self.split * self.level_rows
        self.sources = self.coeffs + excite
        self.first_rows = self.sources + self.box_rows
        self.second_rows = (levels - self.split) * self.level_rows
        self.final = 7 * self.box_rows
        self.third_rows = self.final + excite

    def place_of(self, level):
        return (level if level < self.split else level - self.split) * self.level_rows


def pack(packing, mixing_hbm, sources_hbm, project_hbm, packed, later, sources, project, sems):
    excite = packing.excite
    wide = [
        pltpu.make_async_copy(sources_hbm, sources, sems.at[0]),
        pltpu.make_async_copy(project_hbm, project, sems.at[1]),
    ]
    for copy in wide:
        copy.start()
    rest = [
        pltpu.make_async_copy(
            mixing_hbm.at[pl.ds(0, packing.coeffs)],
            packed.at[pl.ds(0, packing.coeffs)],
            sems.at[2],
        ),
        pltpu.make_async_copy(
            mixing_hbm.at[pl.ds(packing.coeffs, packing.second_rows)], later, sems.at[3]
        ),
    ]
    for block in range(packing.blocks):
        rest.append(
            pltpu.make_async_copy(
                sources_hbm.at[:, pl.ds(block * LANES, LANES)],
                packed.at[pl.ds(packing.sources + block * excite, excite)],
                sems.at[4 + block],
            )
        )
    for copy in rest:
        copy.start()
    for copy in wide:
        copy.wait()
    packed[pl.ds(packing.coeffs, excite)] = jnp.dot(
        sources[...], project[...], preferred_element_type=jnp.float32
    ).astype(jnp.bfloat16)
    for copy in rest:
        copy.wait()


def packed_own(packing, mixing, sources, project):
    vmem = pl.BlockSpec(memory_space=pltpu.VMEM)
    return pl.pallas_call(
        functools.partial(pack, packing),
        name="pack",
        out_shape=tuple(
            pltpu.VMEM((rows, LANES), jnp.bfloat16)
            for rows in (packing.first_rows, packing.second_rows)
        ),
        in_specs=[pl.BlockSpec(memory_space=pl.ANY)] * 3,
        out_specs=(vmem, vmem),
        scratch_shapes=[
            pltpu.VMEM(sources.shape, sources.dtype),
            pltpu.VMEM(project.shape, project.dtype),
            pltpu.SemaphoreType.DMA((4 + packing.blocks,)),
        ],
    )(mixing.reshape(-1, LANES), sources, project)


def first_level(packing, early, coeffs):
    given = [early[box, pl.ds(packing.coeffs, packing.excite)] for box in range(2)]
    for box in range(2):
        pair = jnp.concatenate([given[box], given[1 - box]], axis=1)
        coeffs[box] = jnp.dot(
            pair, early[box, pl.ds(0, packing.level_rows)], preferred_element_type=jnp.float32
        ).astype(coeffs.dtype)


def mixed(packing, level, place, both, blocks):
    axis, apart = place
    upper = lax.axis_index(axis) >> apart & 1
    if level < packing.split:
        blocks = [blocks[0].at[box] for box in range(2)]
    rows = pl.ds(packing.place_of(level), packing.level_rows)
    sums = []
    for box in range(2):
        pair = jnp.concatenate([both[upper, box], both[1 - upper, box]], axis=1)
        sums.append(
            jnp.dot(pair, blocks[box][rows], preferred_element_type=jnp.float32).astype(
                jnp.bfloat16
            )
        )
    return sums


def next_level(packing, level, place, both, *rest):
    *blocks, coeffs = rest
    for box, value in enumerate(mixed(packing, level, place, both, blocks)):
        coeffs[box] = value


def last_level(packing, level, place, both, *rest):
    *blocks, given, final = rest
    given[pl.ds(packing.final, packing.excite)], final[...] = mixed(
        packing, level, place, both, blocks
    )


def in_vmem(kernel, name, out_shape, operands):
    vmem = pl.BlockSpec(memory_space=pltpu.VMEM)
    call = pl.pallas_call(
        kernel,
        name=name,
        out_shape=out_shape,
        in_specs=[vmem] * len(operands),
        out_specs=jax.tree.map(lambda _: vmem, out_shape),
    )
    return call(*(pltpu.with_memory_space_constraint(x, pltpu.VMEM) for x in operands))


def respond(
    packing,
    taken,
    column,
    shared,
    own_final,
    far_expand,
    near_hbm,
    index_hbm,
    response,
    near_blocks,
    around,
    index,
    sems,
):
    excite, rows = packing.excite, packing.box_rows
    targets, positions = index.shape
    block_len = near_blocks.shape[1]
    depth = positions * block_len
    first_of_pair = lax.axis_index("bx") & 1 == 0
    indices = pltpu.make_async_copy(index_hbm, index, sems.at[targets])
    indices.start()
    copies = []
    for target in range(targets):
        part = pl.ds(target * depth, depth)
        copies.append(
            pltpu.make_async_copy(near_hbm.at[part], near_blocks.at[part], sems.at[target])
        )
        copies[-1].start()

    def box_at(x, y):
        if x == 0:
            return column[pl.ds(y * rows, rows)]
        if y == 1 and x < 3:
            return shared[x - 1, pl.ds(packing.sources, rows)]
        return taken[0, pl.ds((3 if y == 1 else x - 1 + 2 * y) * rows, rows)]

    for offset, chosen in enumerate((first_of_pair, jnp.logical_not(first_of_pair))):

        @pl.when(chosen)
        def _():
            for position in range(positions):
                x, y = position // 3, position % 3
                around[pl.ds(position * rows, rows)] = box_at(x + offset, y)

    final = jnp.where(first_of_pair, taken[1, pl.ds(packing.final, excite)], own_final[...])
    indices.wait()
    for target in range(targets):
        picked = []
        for position in range(positions):
            start = position * rows + index[target, position] * excite
            picked.append(around[pl.ds(pl.multiple_of(start, excite), excite)])
        lanes = pl.ds(target * block_len, block_len)
        total = jnp.dot(final, far_expand[:, lanes], preferred_element_type=jnp.float32)
        copies[target].wait()
        blocks = [
            near_blocks[pl.ds(target * depth + position * block_len, block_len)]
            for position in range(positions)
        ]
        total += lax.dot_general(
            jnp.concatenate(picked, axis=1),
            jnp.concatenate(blocks, axis=1),
            (((1,), (1,)), ((), ())),
            preferred_element_type=jnp.float32,
        )
        response[:, 0, 0, lanes] = total


def response_of(packing, taken, column, shared, own_final, far_expand, near_blocks, near_index):
    targets, positions, block_len = near_blocks.shape[:3]
    vmem, hbm = pl.BlockSpec(memory_space=pltpu.VMEM), pl.BlockSpec(memory_space=pl.ANY)
    near_rows = near_blocks.reshape(-1, block_len)
    held = [
        pltpu.with_memory_space_constraint(x, pltpu.VMEM)
        for x in (taken, column, shared, own_final, far_expand)
    ]
    return pl.pallas_call(
        functools.partial(respond, packing),
        name="respond",
        out_shape=jax.ShapeDtypeStruct(
            (packing.excite, 1, 1, far_expand.shape[1]), jnp.float32
        ),
        in_specs=[vmem] * len(held) + [hbm, hbm],
        out_specs=vmem,
        scratch_shapes=[
            pltpu.VMEM(near_rows.shape, near_rows.dtype),
            pltpu.VMEM((positions * packing.box_rows, LANES), column.dtype),
            pltpu.SMEM(near_index.shape, near_index.dtype),
            pltpu.SemaphoreType.DMA((targets + 1,)),
        ],
    )(*held, near_rows, near_index)


def butterfly_levels(packing, levels, blocks, coeffs, first, last):
    rank = LANES
    for level in range(first, last):
        shape = pltpu.VMEM((2, packing.excite, rank), jnp.bfloat16)
        if level == 0:
            coeffs = in_vmem(functools.partial(first_level, packing), "level_0", shape, blocks)
            continue
        place = levels[level]
        both = pair_gather(coeffs, *place)
        kernel = functools.partial(next_level, packing, level, place)
        if level == len(levels) - 1:
            kernel = functools.partial(last_level, packing, level, place)
            shape = (
                pltpu.VMEM((packing.third_rows, LANES), jnp.bfloat16),
                pltpu.VMEM((packing.excite, rank), jnp.bfloat16),
            )
        coeffs = in_vmem(kernel, f"level_{level}", shape, (both, *blocks))
    return coeffs


def per_device(sources, near_blocks, near_index, far_project, far_mixing, far_expand):
    own_sources, own_blocks, own_index = sources[:, 0, 0], near_blocks[0, 0], near_index[0, 0]
    excite, unknowns = own_sources.shape
    rank = far_project.shape[3]
    first_of_pair = lax.axis_index("bx") & 1 == 0
    levels = [("bx", n) for n in range(lax.axis_size("bx").bit_length() - 1)]
    levels += [("by", n) for n in range(lax.axis_size("by").bit_length() - 1)]
    packing = Packing(len(levels), rank, excite, unknowns)
    packed, later = packed_own(packing, far_mixing[0, 0], own_sources, far_project[0, 0])
    shared = pair_gather(packed, "bx", 0)
    later, shared = lax.optimization_barrier((later, shared))
    handed = [(i, i ^ 1) for i in range(0, lax.axis_size("bx"), 2)]
    their_later = lax.ppermute(later, "bx", handed)
    boxes = shared[:, packing.sources :].reshape(2, packing.blocks, excite, LANES)

    def along_first():
        before, after = sent_on(boxes[1], 2, 0), sent_on(boxes[0], -2, 0)
        row = jnp.concatenate([before[None], boxes, after[None]])
        return row, jnp.zeros((2, excite, rank), jnp.bfloat16)

    def levels_early():
        row = jnp.zeros((4, packing.blocks, excite, LANES), jnp.bfloat16)
        return row, butterfly_levels(packing, levels, (shared,), None, 0, packing.split)

    row, coeffs = lax.cond(first_of_pair, along_first, levels_early)
    their_later, coeffs = lax.optimization_barrier((their_later, coeffs))

    def along_second():
        below, above = sent_on(row, 0, 1), sent_on(row, 0, -1)
        given = jnp.concatenate([below[1:], row[3:], above[1:]]).reshape(-1, LANES)
        given = jnp.pad(given, ((0, excite), (0, 0)))
        column = jnp.stack([below[0], row[0], above[0]])
        return column, given, jnp.zeros((excite, rank), jnp.bfloat16)

    def levels_late():
        column = jnp.zeros((3, packing.blocks, excite, LANES), jnp.bfloat16)
        blocks = (their_later, later)
        return column, *butterfly_levels(
            packing, levels, blocks, coeffs, packing.split, len(levels)
        )

    column, given, final = lax.cond(first_of_pair, along_second, levels_late)
    taken = pair_gather(given, "bx", 0)
    return response_of(
        packing,
        taken,
        column.reshape(-1, LANES),
        shared,
        final,
        far_expand[0, 0],
        own_blocks,
        own_index,
    )


def solution(mesh):
    placed = (
        P(None, "bx", "by", None),
        P("bx", "by", None, None, None, None),
        P("bx", "by", None, None),
        P("bx", "by", None, None),
        P("bx", "by", None, None, None, None),
        P("bx", "by", None, None),
    )
    return jax.shard_map(
        per_device, mesh=mesh, in_specs=placed, out_specs=P(None, "bx", "by", None), check_vma=False
    )
```

```python
import functools

import jax
import jax.numpy as jnp
from jax import lax
from jax.experimental import pallas as pl
from jax.experimental.pallas import tpu as pltpu
from jax.sharding import PartitionSpec as P

BOTH = ("bx", "by")
LANES = 128


def pair_gather(values, axis, apart):
    count = lax.axis_size(axis)
    pairs = [[i, i ^ 1 << apart] for i in range(count) if not i >> apart & 1]
    return lax.all_gather(values, axis, axis_index_groups=pairs)


def sent_on(values, step_x, step_y):
    count_x, count_y = lax.axis_size("bx"), lax.axis_size("by")
    moves = []
    for x in range(0, count_x, 2):
        for y in range(count_y):
            to_x, to_y = x + step_x, y + step_y
            if 0 <= to_x < count_x and 0 <= to_y < count_y:
                moves.append((x * count_y + y, to_x * count_y + to_y))
    return lax.ppermute(values, BOTH, moves)


class Packing:
    def __init__(self, levels, rank, excite, unknowns):
        self.excite, self.blocks = excite, unknowns // LANES
        self.split = 2
        self.level_rows = 2 * rank
        self.box_rows = self.blocks * excite
        self.coeffs = self.split * self.level_rows
        self.sources = self.coeffs + excite
        self.first_rows = self.sources + self.box_rows
        self.second_rows = (levels - self.split) * self.level_rows
        self.final = 7 * self.box_rows
        self.third_rows = self.final + excite

    def place_of(self, level):
        return (level if level < self.split else level - self.split) * self.level_rows


def pack(packing, mixing_hbm, sources_hbm, project_hbm, packed, later, sources, project, sems):
    excite = packing.excite
    wide = [
        pltpu.make_async_copy(sources_hbm, sources, sems.at[0]),
        pltpu.make_async_copy(project_hbm, project, sems.at[1]),
    ]
    for copy in wide:
        copy.start()
    rest = [
        pltpu.make_async_copy(
            mixing_hbm.at[pl.ds(0, packing.coeffs)],
            packed.at[pl.ds(0, packing.coeffs)],
            sems.at[2],
        ),
        pltpu.make_async_copy(
            mixing_hbm.at[pl.ds(packing.coeffs, packing.second_rows)], later, sems.at[3]
        ),
    ]
    for block in range(packing.blocks):
        rest.append(
            pltpu.make_async_copy(
                sources_hbm.at[:, pl.ds(block * LANES, LANES)],
                packed.at[pl.ds(packing.sources + block * excite, excite)],
                sems.at[4 + block],
            )
        )
    for copy in rest:
        copy.start()
    for copy in wide:
        copy.wait()
    packed[pl.ds(packing.coeffs, excite)] = jnp.dot(
        sources[...], project[...], preferred_element_type=jnp.float32
    ).astype(jnp.bfloat16)
    for copy in rest:
        copy.wait()


def packed_own(packing, mixing, sources, project):
    vmem = pl.BlockSpec(memory_space=pltpu.VMEM)
    return pl.pallas_call(
        functools.partial(pack, packing),
        name="pack",
        out_shape=tuple(
            pltpu.VMEM((rows, LANES), jnp.bfloat16)
            for rows in (packing.first_rows, packing.second_rows)
        ),
        in_specs=[pl.BlockSpec(memory_space=pl.ANY)] * 3,
        out_specs=(vmem, vmem),
        scratch_shapes=[
            pltpu.VMEM(sources.shape, sources.dtype),
            pltpu.VMEM(project.shape, project.dtype),
            pltpu.SemaphoreType.DMA((4 + packing.blocks,)),
        ],
    )(mixing.reshape(-1, LANES), sources, project)


def first_level(packing, early, coeffs):
    given = [early[box, pl.ds(packing.coeffs, packing.excite)] for box in range(2)]
    for box in range(2):
        pair = jnp.concatenate([given[box], given[1 - box]], axis=1)
        coeffs[box] = jnp.dot(
            pair, early[box, pl.ds(0, packing.level_rows)], preferred_element_type=jnp.float32
        ).astype(coeffs.dtype)


def mixed(packing, level, place, both, blocks):
    axis, apart = place
    upper = lax.axis_index(axis) >> apart & 1
    if level < packing.split:
        blocks = [blocks[0].at[box] for box in range(2)]
    rows = pl.ds(packing.place_of(level), packing.level_rows)
    sums = []
    for box in range(2):
        pair = jnp.concatenate([both[upper, box], both[1 - upper, box]], axis=1)
        sums.append(
            jnp.dot(pair, blocks[box][rows], preferred_element_type=jnp.float32).astype(
                jnp.bfloat16
            )
        )
    return sums


def next_level(packing, level, place, both, *rest):
    *blocks, coeffs = rest
    for box, value in enumerate(mixed(packing, level, place, both, blocks)):
        coeffs[box] = value


def last_level(packing, level, place, both, *rest):
    *blocks, given, final = rest
    given[pl.ds(packing.final, packing.excite)], final[...] = mixed(
        packing, level, place, both, blocks
    )


def in_vmem(kernel, name, out_shape, operands):
    vmem = pl.BlockSpec(memory_space=pltpu.VMEM)
    call = pl.pallas_call(
        kernel,
        name=name,
        out_shape=out_shape,
        in_specs=[vmem] * len(operands),
        out_specs=jax.tree.map(lambda _: vmem, out_shape),
    )
    return call(*(pltpu.with_memory_space_constraint(x, pltpu.VMEM) for x in operands))


def respond(
    packing,
    taken,
    column,
    shared,
    own_final,
    far_expand,
    near_hbm,
    index_hbm,
    response_hbm,
    response,
    near_blocks,
    around,
    index,
    sems,
):
    excite, rows = packing.excite, packing.box_rows
    targets, positions = index.shape
    block_len = near_blocks.shape[1]
    depth = positions * block_len
    first_of_pair = lax.axis_index("bx") & 1 == 0
    indices = pltpu.make_async_copy(index_hbm, index, sems.at[targets])
    indices.start()
    copies = []
    for target in range(targets):
        part = pl.ds(target * depth, depth)
        copies.append(
            pltpu.make_async_copy(near_hbm.at[part], near_blocks.at[part], sems.at[target])
        )
        copies[-1].start()

    def box_at(x, y):
        if x == 0:
            return column[pl.ds(y * rows, rows)]
        if y == 1 and x < 3:
            return shared[x - 1, pl.ds(packing.sources, rows)]
        return taken[0, pl.ds((3 if y == 1 else x - 1 + 2 * y) * rows, rows)]

    for offset, chosen in enumerate((first_of_pair, jnp.logical_not(first_of_pair))):

        @pl.when(chosen)
        def _():
            for position in range(positions):
                x, y = position // 3, position % 3
                around[pl.ds(position * rows, rows)] = box_at(x + offset, y)

    final = jnp.where(first_of_pair, taken[1, pl.ds(packing.final, excite)], own_final[...])
    indices.wait()
    written = []
    for target in range(targets):
        picked = []
        for position in range(positions):
            start = position * rows + index[target, position] * excite
            picked.append(around[pl.ds(pl.multiple_of(start, excite), excite)])
        lanes = pl.ds(target * block_len, block_len)
        total = jnp.dot(final, far_expand[:, lanes], preferred_element_type=jnp.float32)
        copies[target].wait()
        blocks = [
            near_blocks[pl.ds(target * depth + position * block_len, block_len)]
            for position in range(positions)
        ]
        total += lax.dot_general(
            jnp.concatenate(picked, axis=1),
            jnp.concatenate(blocks, axis=1),
            (((1,), (1,)), ((), ())),
            preferred_element_type=jnp.float32,
        )
        response[:, 0, 0, lanes] = total
        part = response.at[:, :, :, lanes], response_hbm.at[:, :, :, lanes]
        written.append(pltpu.make_async_copy(*part, sems.at[targets + 1 + target]))
        written[-1].start()
    for copy in written:
        copy.wait()


def response_of(packing, taken, column, shared, own_final, far_expand, near_blocks, near_index):
    targets, positions, block_len = near_blocks.shape[:3]
    vmem, hbm = pl.BlockSpec(memory_space=pltpu.VMEM), pl.BlockSpec(memory_space=pl.ANY)
    shape = (packing.excite, 1, 1, far_expand.shape[1])
    near_rows = near_blocks.reshape(-1, block_len)
    held = [
        pltpu.with_memory_space_constraint(x, pltpu.VMEM)
        for x in (taken, column, shared, own_final, far_expand)
    ]
    return pl.pallas_call(
        functools.partial(respond, packing),
        name="respond",
        out_shape=jax.ShapeDtypeStruct(shape, jnp.float32),
        in_specs=[vmem] * len(held) + [hbm, hbm],
        out_specs=hbm,
        scratch_shapes=[
            pltpu.VMEM(shape, jnp.float32),
            pltpu.VMEM(near_rows.shape, near_rows.dtype),
            pltpu.VMEM((positions * packing.box_rows, LANES), column.dtype),
            pltpu.SMEM(near_index.shape, near_index.dtype),
            pltpu.SemaphoreType.DMA((2 * targets + 1,)),
        ],
    )(*held, near_rows, near_index)


def butterfly_levels(packing, levels, blocks, coeffs, first, last):
    rank = LANES
    for level in range(first, last):
        shape = pltpu.VMEM((2, packing.excite, rank), jnp.bfloat16)
        if level == 0:
            coeffs = in_vmem(functools.partial(first_level, packing), "level_0", shape, blocks)
            continue
        place = levels[level]
        both = pair_gather(coeffs, *place)
        kernel = functools.partial(next_level, packing, level, place)
        if level == len(levels) - 1:
            kernel = functools.partial(last_level, packing, level, place)
            shape = (
                pltpu.VMEM((packing.third_rows, LANES), jnp.bfloat16),
                pltpu.VMEM((packing.excite, rank), jnp.bfloat16),
            )
        coeffs = in_vmem(kernel, f"level_{level}", shape, (both, *blocks))
    return coeffs


def per_device(sources, near_blocks, near_index, far_project, far_mixing, far_expand):
    own_sources, own_blocks, own_index = sources[:, 0, 0], near_blocks[0, 0], near_index[0, 0]
    excite, unknowns = own_sources.shape
    rank = far_project.shape[3]
    first_of_pair = lax.axis_index("bx") & 1 == 0
    levels = [("bx", n) for n in range(lax.axis_size("bx").bit_length() - 1)]
    levels += [("by", n) for n in range(lax.axis_size("by").bit_length() - 1)]
    packing = Packing(len(levels), rank, excite, unknowns)
    packed, later = packed_own(packing, far_mixing[0, 0], own_sources, far_project[0, 0])
    shared = pair_gather(packed, "bx", 0)
    later, shared = lax.optimization_barrier((later, shared))
    handed = [(i, i ^ 1) for i in range(0, lax.axis_size("bx"), 2)]
    their_later = lax.ppermute(later, "bx", handed)
    boxes = shared[:, packing.sources :].reshape(2, packing.blocks, excite, LANES)

    def along_first():
        before, after = sent_on(boxes[1], 2, 0), sent_on(boxes[0], -2, 0)
        row = jnp.concatenate([before[None], boxes, after[None]])
        return row, jnp.zeros((2, excite, rank), jnp.bfloat16)

    def levels_early():
        row = jnp.zeros((4, packing.blocks, excite, LANES), jnp.bfloat16)
        return row, butterfly_levels(packing, levels, (shared,), None, 0, packing.split)

    row, coeffs = lax.cond(first_of_pair, along_first, levels_early)
    their_later, coeffs = lax.optimization_barrier((their_later, coeffs))

    def along_second():
        below, above = sent_on(row, 0, 1), sent_on(row, 0, -1)
        given = jnp.concatenate([below[1:], row[3:], above[1:]]).reshape(-1, LANES)
        given = jnp.pad(given, ((0, excite), (0, 0)))
        column = jnp.stack([below[0], row[0], above[0]])
        return column, given, jnp.zeros((excite, rank), jnp.bfloat16)

    def levels_late():
        column = jnp.zeros((3, packing.blocks, excite, LANES), jnp.bfloat16)
        blocks = (their_later, later)
        return column, *butterfly_levels(
            packing, levels, blocks, coeffs, packing.split, len(levels)
        )

    column, given, final = lax.cond(first_of_pair, along_second, levels_late)
    taken = pair_gather(given, "bx", 0)
    return response_of(
        packing,
        taken,
        column.reshape(-1, LANES),
        shared,
        final,
        far_expand[0, 0],
        own_blocks,
        own_index,
    )


def solution(mesh):
    placed = (
        P(None, "bx", "by", None),
        P("bx", "by", None, None, None, None),
        P("bx", "by", None, None),
        P("bx", "by", None, None),
        P("bx", "by", None, None, None, None),
        P("bx", "by", None, None),
    )
    return jax.shard_map(
        per_device, mesh=mesh, in_specs=placed, out_specs=P(None, "bx", "by", None), check_vma=False
    )
```

```python
import functools

import jax
import jax.numpy as jnp
from jax import lax
from jax.experimental import pallas as pl
from jax.experimental.pallas import tpu as pltpu
from jax.sharding import PartitionSpec as P

BOTH = ("bx", "by")
LANES = 128
GRANT = pltpu.CompilerParams(vmem_limit_bytes=8 << 20)


def pair_gather(values, axis, apart):
    count = lax.axis_size(axis)
    pairs = [[i, i ^ 1 << apart] for i in range(count) if not i >> apart & 1]
    return lax.all_gather(values, axis, axis_index_groups=pairs)


def sent_on(values, step_x, step_y):
    count_x, count_y = lax.axis_size("bx"), lax.axis_size("by")
    moves = []
    for x in range(0, count_x, 2):
        for y in range(count_y):
            to_x, to_y = x + step_x, y + step_y
            if 0 <= to_x < count_x and 0 <= to_y < count_y:
                moves.append((x * count_y + y, to_x * count_y + to_y))
    return lax.ppermute(values, BOTH, moves)


class Packing:
    def __init__(self, levels, rank, excite, unknowns):
        self.excite, self.blocks = excite, unknowns // LANES
        self.split = levels - 3
        self.level_rows = 2 * rank
        self.box_rows = self.blocks * excite
        self.coeffs = self.split * self.level_rows
        self.sources = self.coeffs + excite
        self.first_rows = self.sources + self.box_rows
        self.late_rows = (levels - self.split) * self.level_rows
        self.late = 7 * self.box_rows
        self.second_rows = self.late + self.late_rows

    def place_of(self, level):
        return (level if level < self.split else level - self.split) * self.level_rows


def pack(packing, mixing_hbm, sources_hbm, project_hbm, packed, later, sources, project, sems):
    excite = packing.excite
    wide = [
        pltpu.make_async_copy(sources_hbm, sources, sems.at[0]),
        pltpu.make_async_copy(project_hbm, project, sems.at[1]),
    ]
    for copy in wide:
        copy.start()
    rest = [
        pltpu.make_async_copy(
            mixing_hbm.at[pl.ds(0, packing.coeffs)],
            packed.at[pl.ds(0, packing.coeffs)],
            sems.at[2],
        ),
        pltpu.make_async_copy(
            mixing_hbm.at[pl.ds(packing.coeffs, packing.late_rows)], later, sems.at[3]
        ),
    ]
    for block in range(packing.blocks):
        rest.append(
            pltpu.make_async_copy(
                sources_hbm.at[:, pl.ds(block * LANES, LANES)],
                packed.at[pl.ds(packing.sources + block * excite, excite)],
                sems.at[4 + block],
            )
        )
    for copy in rest:
        copy.start()
    for copy in wide:
        copy.wait()
    packed[pl.ds(packing.coeffs, excite)] = jnp.dot(
        sources[...], project[...], preferred_element_type=jnp.float32
    ).astype(jnp.bfloat16)
    for copy in rest:
        copy.wait()


def packed_own(packing, mixing, sources, project):
    vmem = pl.BlockSpec(memory_space=pltpu.VMEM)
    operands = (mixing.reshape(-1, LANES), sources, project)
    return pl.pallas_call(
        functools.partial(pack, packing),
        name="pack",
        compiler_params=GRANT,
        out_shape=tuple(
            pltpu.VMEM((rows, LANES), jnp.bfloat16)
            for rows in (packing.first_rows, packing.late_rows)
        ),
        in_specs=[pl.BlockSpec(memory_space=pl.ANY)] * 3,
        out_specs=(vmem, vmem),
        scratch_shapes=[
            pltpu.VMEM(sources.shape, sources.dtype),
            pltpu.VMEM(project.shape, project.dtype),
            pltpu.SemaphoreType.DMA((4 + packing.blocks,)),
        ],
    )(*(pltpu.with_memory_space_constraint(x, pltpu.HBM) for x in operands))


def first_level(packing, early, coeffs):
    given = [early[box, pl.ds(packing.coeffs, packing.excite)] for box in range(2)]
    for box in range(2):
        pair = jnp.concatenate([given[box], given[1 - box]], axis=1)
        coeffs[box] = jnp.dot(
            pair, early[box, pl.ds(0, packing.level_rows)], preferred_element_type=jnp.float32
        ).astype(coeffs.dtype)


def mixed(packing, level, place, both, blocks):
    axis, apart = place
    upper = lax.axis_index(axis) >> apart & 1
    if level < packing.split:
        blocks = [blocks[0].at[box] for box in range(2)]
        starts = [packing.place_of(level)] * 2
    else:
        starts = [packing.late + packing.place_of(level), packing.place_of(level)]
    sums = []
    for box in range(2):
        pair = jnp.concatenate([both[upper, box], both[1 - upper, box]], axis=1)
        weights = blocks[box][pl.ds(starts[box], packing.level_rows)]
        sums.append(
            jnp.dot(pair, weights, preferred_element_type=jnp.float32).astype(jnp.bfloat16)
        )
    return sums


def next_level(packing, level, place, both, *rest):
    blocks = rest[: 1 if level < packing.split else 2]
    coeffs = rest[len(blocks)]
    for box, value in enumerate(mixed(packing, level, place, both, blocks)):
        coeffs[box] = value


def last_level(packing, level, place, both, theirs, own, given, final):
    given[...], final[...] = mixed(packing, level, place, both, (theirs, own))


def in_vmem(kernel, name, out_shape, operands):
    vmem = pl.BlockSpec(memory_space=pltpu.VMEM)
    call = pl.pallas_call(
        kernel,
        name=name,
        compiler_params=GRANT,
        out_shape=out_shape,
        in_specs=[vmem] * len(operands),
        out_specs=jax.tree.map(lambda _: vmem, out_shape),
    )
    return call(*(pltpu.with_memory_space_constraint(x, pltpu.VMEM) for x in operands))


def near_field(
    packing, offset, beside, shared, *rest
):
    column, (near_blocks, index_ref, near, index, sem) = rest[:-5], rest[-5:]
    excite, rows = packing.excite, packing.box_rows
    targets, positions = index.shape
    block_len = near_blocks.shape[1]
    indices = pltpu.make_async_copy(index_ref, index, sem)
    indices.start()
    indices.wait()

    def block_at(x, y, block):
        at = pl.multiple_of(block * excite, excite)
        if x == 0:
            return column[0][pl.ds(y * rows + at, excite)]
        if y == 1 and x < 3:
            return shared[x - 1, pl.ds(packing.sources + at, excite)]
        return beside[pl.ds((3 if y == 1 else x - 1 + 2 * y) * rows + at, excite)]

    for target in range(targets):
        picked, blocks = [], []
        for position in range(positions):
            x, y = position // 3 + offset, position % 3
            picked.append(block_at(x, y, index[target, position]))
            start = (target * positions + position) * block_len
            blocks.append(near_blocks[pl.ds(start, block_len)])
        near[:, pl.ds(target * block_len, block_len)] = lax.dot_general(
            jnp.concatenate(picked, axis=1),
            jnp.concatenate(blocks, axis=1),
            (((1,), (1,)), ((), ())),
            preferred_element_type=jnp.float32,
        )


def near_of(packing, offset, beside, shared, column, near_blocks, near_index):
    vmem = pl.BlockSpec(memory_space=pltpu.VMEM)
    around = (beside, shared, *column)
    operands = [pltpu.with_memory_space_constraint(x, pltpu.VMEM) for x in around]
    operands += [near_blocks.reshape(-1, near_blocks.shape[3]), near_index]
    return pl.pallas_call(
        functools.partial(near_field, packing, offset),
        name=f"near_{offset}",
        compiler_params=GRANT,
        out_shape=pltpu.VMEM((packing.excite, packing.blocks * LANES), jnp.float32),
        in_specs=[vmem] * len(operands),
        out_specs=vmem,
        scratch_shapes=[
            pltpu.SMEM(near_index.shape, near_index.dtype),
            pltpu.SemaphoreType.DMA,
        ],
    )(*operands)


def respond(taken, own_final, near, far_expand, response_hbm, response, sems):
    first_of_pair = lax.axis_index("bx") & 1 == 0
    final = jnp.where(first_of_pair, taken[1], own_final[...])
    width = response.shape[3] // sems.shape[0]
    copies = []
    for part in range(sems.shape[0]):
        lanes = pl.ds(part * width, width)
        response[:, 0, 0, lanes] = near[:, lanes] + jnp.dot(
            final, far_expand[:, lanes], preferred_element_type=jnp.float32
        )
        ends = response.at[:, :, :, lanes], response_hbm.at[:, :, :, lanes]
        copies.append(pltpu.make_async_copy(*ends, sems.at[part]))
        copies[-1].start()
    for copy in copies:
        copy.wait()


def response_of(taken, final, near, far_expand):
    vmem = pl.BlockSpec(memory_space=pltpu.VMEM)
    shape = (near.shape[0], 1, 1, near.shape[1])
    held = [pltpu.with_memory_space_constraint(x, pltpu.VMEM) for x in (taken, final, near)]
    return pl.pallas_call(
        respond,
        name="respond",
        compiler_params=GRANT,
        out_shape=jax.ShapeDtypeStruct(shape, jnp.float32),
        in_specs=[vmem] * 4,
        out_specs=pl.BlockSpec(memory_space=pl.ANY),
        scratch_shapes=[pltpu.VMEM(shape, jnp.float32), pltpu.SemaphoreType.DMA((4,))],
    )(*held, far_expand)


def per_device(sources, near_blocks, near_index, far_project, far_mixing, far_expand):
    own_sources, own_blocks, own_index = sources[:, 0, 0], near_blocks[0, 0], near_index[0, 0]
    excite, unknowns = own_sources.shape
    rank = far_project.shape[3]
    first_of_pair = lax.axis_index("bx") & 1 == 0
    levels = [("bx", n) for n in range(lax.axis_size("bx").bit_length() - 1)]
    levels += [("by", n) for n in range(lax.axis_size("by").bit_length() - 1)]
    packing = Packing(len(levels), rank, excite, unknowns)
    packed, later = packed_own(packing, far_mixing[0, 0], own_sources, far_project[0, 0])
    shared = pair_gather(packed, "bx", 0)
    coeffs_shape = pltpu.VMEM((2, excite, rank), jnp.bfloat16)
    column_shape = pltpu.VMEM((3 * packing.box_rows, LANES), jnp.bfloat16)
    given_shape = pltpu.VMEM((packing.second_rows, LANES), jnp.bfloat16)

    def gathering():
        boxes = shared[:, packing.sources :].reshape(2, packing.blocks, excite, LANES)
        before, after = sent_on(boxes[1], 2, 0), sent_on(boxes[0], -2, 0)
        row = jnp.concatenate([before[None], boxes, after[None]])
        below, above = sent_on(row, 0, 1), sent_on(row, 0, -1)
        given = jnp.concatenate([below[1:], row[3:], above[1:]]).reshape(-1, LANES)
        column = jnp.stack([below[0], row[0], above[0]]).reshape(-1, LANES)
        return jnp.zeros((2, excite, rank), jnp.bfloat16), jnp.concatenate([given, later]), column

    def levels_early():
        coeffs = in_vmem(functools.partial(first_level, packing), "level_0", coeffs_shape, (shared,))
        for level in range(1, packing.split):
            shape = coeffs_shape
            if level == packing.split - 1:
                shape = (coeffs_shape, given_shape, column_shape)
            both = pair_gather(coeffs, *levels[level])
            kernel = functools.partial(next_level, packing, level, levels[level])
            coeffs = in_vmem(kernel, f"level_{level}", shape, (both, shared))
        return tuple(coeffs)

    coeffs, given, column = lax.cond(first_of_pair, gathering, levels_early)
    handed = lax.ppermute(given, "bx", [(i, i ^ 1) for i in range(0, lax.axis_size("bx"), 2)])
    both = lax.cond(
        first_of_pair,
        lambda: jnp.stack([coeffs, coeffs]),
        lambda: pair_gather(coeffs, *levels[packing.split]),
    )

    def near_only():
        near = near_of(packing, 0, given, shared, (column,), own_blocks, own_index)
        return near, coeffs[0], coeffs[1]

    def levels_late():
        gathered = both
        for level in range(packing.split, len(levels)):
            kernel = functools.partial(next_level, packing, level, levels[level])
            shape = coeffs_shape
            if level == len(levels) - 1:
                kernel = functools.partial(last_level, packing, level, levels[level])
                shape = (pltpu.VMEM((excite, rank), jnp.bfloat16),) * 2
            result = in_vmem(kernel, f"level_{level}", shape, (gathered, handed, later))
            if level < len(levels) - 1:
                gathered = pair_gather(result, *levels[level + 1])
        beside, result = lax.optimization_barrier((handed, tuple(result)))
        near = near_of(packing, 1, beside, shared, (), own_blocks, own_index)
        return near, *result

    near, final_given, final = lax.cond(first_of_pair, near_only, levels_late)
    taken = pair_gather(final_given, "bx", 0)
    return response_of(taken, final, near, far_expand[0, 0])


def solution(mesh):
    placed = (
        P(None, "bx", "by", None),
        P("bx", "by", None, None, None, None),
        P("bx", "by", None, None),
        P("bx", "by", None, None),
        P("bx", "by", None, None, None, None),
        P("bx", "by", None, None),
    )
    return jax.shard_map(
        per_device, mesh=mesh, in_specs=placed, out_specs=P(None, "bx", "by", None), check_vma=False
    )
```

```python
import functools

import jax
import jax.numpy as jnp
from jax import lax
from jax.experimental import pallas as pl
from jax.experimental.pallas import tpu as pltpu
from jax.sharding import PartitionSpec as P

BOTH = ("bx", "by")
LANES = 128
GRANT = pltpu.CompilerParams(vmem_limit_bytes=8 << 20)


def pair_gather(values, axis, apart):
    count = lax.axis_size(axis)
    pairs = [[i, i ^ 1 << apart] for i in range(count) if not i >> apart & 1]
    return lax.all_gather(values, axis, axis_index_groups=pairs)


def swapped(values, axis, phase):
    count_x, count_y = lax.axis_size("bx"), lax.axis_size("by")
    moves = []
    for x in range(0, count_x, 2):
        for y in range(count_y):
            place, count = (x // 2, count_x // 2) if axis == "bx" else (y, count_y)
            other = place + (1 if place % 2 == phase else -1)
            if 0 <= other < count:
                target = 2 * other * count_y + y if axis == "bx" else x * count_y + other
                moves.append((x * count_y + y, target))
    return lax.ppermute(values, BOTH, moves)


def surroundings(boxes):
    even = lax.axis_index("bx") >> 1 & 1 == 0
    first = swapped(jnp.where(even, boxes[1], boxes[0]), "bx", 0)
    second = swapped(jnp.where(even, boxes[0], boxes[1]), "bx", 1)
    before, after = jnp.where(even, second, first), jnp.where(even, first, second)
    row = jnp.concatenate([before[None], boxes, after[None]])
    even = lax.axis_index("by") & 1 == 0
    first, second = swapped(row, "by", 0), swapped(row, "by", 1)
    return jnp.where(even, second, first), row, jnp.where(even, first, second)


class Packing:
    def __init__(self, levels, rank, excite, unknowns):
        self.excite, self.blocks = excite, unknowns // LANES
        self.split = levels - 3
        self.level_rows = 2 * rank
        self.box_rows = self.blocks * excite
        self.coeffs = self.split * self.level_rows
        self.sources = self.coeffs + excite
        self.first_rows = self.sources + self.box_rows
        self.late_rows = (levels - self.split) * self.level_rows
        self.late = 7 * self.box_rows
        self.second_rows = self.late + self.late_rows

    def place_of(self, level):
        return (level if level < self.split else level - self.split) * self.level_rows


def pack(packing, mixing_hbm, sources_hbm, project_hbm, packed, later, sources, project, sems):
    excite = packing.excite
    wide = [
        pltpu.make_async_copy(sources_hbm, sources, sems.at[0]),
        pltpu.make_async_copy(project_hbm, project, sems.at[1]),
    ]
    for copy in wide:
        copy.start()
    rest = [
        pltpu.make_async_copy(
            mixing_hbm.at[pl.ds(0, packing.coeffs)],
            packed.at[pl.ds(0, packing.coeffs)],
            sems.at[2],
        ),
        pltpu.make_async_copy(
            mixing_hbm.at[pl.ds(packing.coeffs, packing.late_rows)], later, sems.at[3]
        ),
    ]
    for block in range(packing.blocks):
        rest.append(
            pltpu.make_async_copy(
                sources_hbm.at[:, pl.ds(block * LANES, LANES)],
                packed.at[pl.ds(packing.sources + block * excite, excite)],
                sems.at[4 + block],
            )
        )
    for copy in rest:
        copy.start()
    for copy in wide:
        copy.wait()
    packed[pl.ds(packing.coeffs, excite)] = jnp.dot(
        sources[...], project[...], preferred_element_type=jnp.float32
    ).astype(jnp.bfloat16)
    for copy in rest:
        copy.wait()


def packed_own(packing, mixing, sources, project):
    vmem = pl.BlockSpec(memory_space=pltpu.VMEM)
    operands = (mixing.reshape(-1, LANES), sources, project)
    return pl.pallas_call(
        functools.partial(pack, packing),
        name="pack",
        compiler_params=GRANT,
        out_shape=tuple(
            pltpu.VMEM((rows, LANES), jnp.bfloat16)
            for rows in (packing.first_rows, packing.late_rows)
        ),
        in_specs=[pl.BlockSpec(memory_space=pl.ANY)] * 3,
        out_specs=(vmem, vmem),
        scratch_shapes=[
            pltpu.VMEM(sources.shape, sources.dtype),
            pltpu.VMEM(project.shape, project.dtype),
            pltpu.SemaphoreType.DMA((4 + packing.blocks,)),
        ],
    )(*(pltpu.with_memory_space_constraint(x, pltpu.HBM) for x in operands))


def first_level(packing, early, coeffs):
    given = [early[box, pl.ds(packing.coeffs, packing.excite)] for box in range(2)]
    for box in range(2):
        pair = jnp.concatenate([given[box], given[1 - box]], axis=1)
        coeffs[box] = jnp.dot(
            pair, early[box, pl.ds(0, packing.level_rows)], preferred_element_type=jnp.float32
        ).astype(coeffs.dtype)


def mixed(packing, level, place, both, blocks):
    axis, apart = place
    upper = lax.axis_index(axis) >> apart & 1
    if level < packing.split:
        blocks = [blocks[0].at[box] for box in range(2)]
        starts = [packing.place_of(level)] * 2
    else:
        starts = [packing.late + packing.place_of(level), packing.place_of(level)]
    sums = []
    for box in range(2):
        pair = jnp.concatenate([both[upper, box], both[1 - upper, box]], axis=1)
        weights = blocks[box][pl.ds(starts[box], packing.level_rows)]
        sums.append(
            jnp.dot(pair, weights, preferred_element_type=jnp.float32).astype(jnp.bfloat16)
        )
    return sums


def next_level(packing, level, place, both, *rest):
    blocks = rest[: 1 if level < packing.split else 2]
    coeffs = rest[len(blocks)]
    for box, value in enumerate(mixed(packing, level, place, both, blocks)):
        coeffs[box] = value


def last_level(packing, level, place, both, theirs, own, given, final):
    given[...], final[...] = mixed(packing, level, place, both, (theirs, own))


def in_vmem(kernel, name, out_shape, operands):
    vmem = pl.BlockSpec(memory_space=pltpu.VMEM)
    call = pl.pallas_call(
        kernel,
        name=name,
        compiler_params=GRANT,
        out_shape=out_shape,
        in_specs=[vmem] * len(operands),
        out_specs=jax.tree.map(lambda _: vmem, out_shape),
    )
    return call(*(pltpu.with_memory_space_constraint(x, pltpu.VMEM) for x in operands))


def near_field(
    packing, offset, beside, shared, *rest
):
    column, (near_blocks, index_ref, near, index, sem) = rest[:-5], rest[-5:]
    excite, rows = packing.excite, packing.box_rows
    targets, positions = index.shape
    block_len = near_blocks.shape[1]
    indices = pltpu.make_async_copy(index_ref, index, sem)
    indices.start()
    indices.wait()

    def block_at(x, y, block):
        at = pl.multiple_of(block * excite, excite)
        if x == 0:
            return column[0][pl.ds(y * rows + at, excite)]
        if y == 1 and x < 3:
            return shared[x - 1, pl.ds(packing.sources + at, excite)]
        return beside[pl.ds((3 if y == 1 else x - 1 + 2 * y) * rows + at, excite)]

    for target in range(targets):
        picked, blocks = [], []
        for position in range(positions):
            x, y = position // 3 + offset, position % 3
            picked.append(block_at(x, y, index[target, position]))
            start = (target * positions + position) * block_len
            blocks.append(near_blocks[pl.ds(start, block_len)])
        near[:, pl.ds(target * block_len, block_len)] = lax.dot_general(
            jnp.concatenate(picked, axis=1),
            jnp.concatenate(blocks, axis=1),
            (((1,), (1,)), ((), ())),
            preferred_element_type=jnp.float32,
        )


def near_of(packing, offset, beside, shared, column, near_blocks, near_index):
    vmem = pl.BlockSpec(memory_space=pltpu.VMEM)
    around = (beside, shared, *column)
    operands = [pltpu.with_memory_space_constraint(x, pltpu.VMEM) for x in around]
    operands += [near_blocks.reshape(-1, near_blocks.shape[3]), near_index]
    return pl.pallas_call(
        functools.partial(near_field, packing, offset),
        name=f"near_{offset}",
        compiler_params=GRANT,
        out_shape=pltpu.VMEM((packing.excite, packing.blocks * LANES), jnp.float32),
        in_specs=[vmem] * len(operands),
        out_specs=vmem,
        scratch_shapes=[
            pltpu.SMEM(near_index.shape, near_index.dtype),
            pltpu.SemaphoreType.DMA,
        ],
    )(*operands)


def respond(taken, own_final, near, far_expand, response_hbm, response, sems):
    first_of_pair = lax.axis_index("bx") & 1 == 0
    final = jnp.where(first_of_pair, taken[1], own_final[...])
    width = response.shape[3] // sems.shape[0]
    copies = []
    for part in range(sems.shape[0]):
        lanes = pl.ds(part * width, width)
        response[:, 0, 0, lanes] = near[:, lanes] + jnp.dot(
            final, far_expand[:, lanes], preferred_element_type=jnp.float32
        )
        ends = response.at[:, :, :, lanes], response_hbm.at[:, :, :, lanes]
        copies.append(pltpu.make_async_copy(*ends, sems.at[part]))
        copies[-1].start()
    for copy in copies:
        copy.wait()


def response_of(taken, final, near, far_expand):
    vmem = pl.BlockSpec(memory_space=pltpu.VMEM)
    shape = (near.shape[0], 1, 1, near.shape[1])
    held = [pltpu.with_memory_space_constraint(x, pltpu.VMEM) for x in (taken, final, near)]
    return pl.pallas_call(
        respond,
        name="respond",
        compiler_params=GRANT,
        out_shape=jax.ShapeDtypeStruct(shape, jnp.float32),
        in_specs=[vmem] * 4,
        out_specs=pl.BlockSpec(memory_space=pl.ANY),
        scratch_shapes=[pltpu.VMEM(shape, jnp.float32), pltpu.SemaphoreType.DMA((4,))],
    )(*held, far_expand)


def per_device(sources, near_blocks, near_index, far_project, far_mixing, far_expand):
    own_sources, own_blocks, own_index = sources[:, 0, 0], near_blocks[0, 0], near_index[0, 0]
    excite, unknowns = own_sources.shape
    rank = far_project.shape[3]
    first_of_pair = lax.axis_index("bx") & 1 == 0
    levels = [("bx", n) for n in range(lax.axis_size("bx").bit_length() - 1)]
    levels += [("by", n) for n in range(lax.axis_size("by").bit_length() - 1)]
    packing = Packing(len(levels), rank, excite, unknowns)
    packed, later = packed_own(packing, far_mixing[0, 0], own_sources, far_project[0, 0])
    shared = pair_gather(packed, "bx", 0)
    coeffs_shape = pltpu.VMEM((2, excite, rank), jnp.bfloat16)
    column_shape = pltpu.VMEM((3 * packing.box_rows, LANES), jnp.bfloat16)
    given_shape = pltpu.VMEM((packing.second_rows, LANES), jnp.bfloat16)

    def gathering():
        boxes = shared[:, packing.sources :].reshape(2, packing.blocks, excite, LANES)
        below, row, above = surroundings(boxes)
        given = jnp.concatenate([below[1:], row[3:], above[1:]]).reshape(-1, LANES)
        column = jnp.stack([below[0], row[0], above[0]]).reshape(-1, LANES)
        return jnp.zeros((2, excite, rank), jnp.bfloat16), jnp.concatenate([given, later]), column

    def levels_early():
        coeffs = in_vmem(functools.partial(first_level, packing), "level_0", coeffs_shape, (shared,))
        for level in range(1, packing.split):
            shape = coeffs_shape
            if level == packing.split - 1:
                shape = (coeffs_shape, given_shape, column_shape)
            both = pair_gather(coeffs, *levels[level])
            kernel = functools.partial(next_level, packing, level, levels[level])
            coeffs = in_vmem(kernel, f"level_{level}", shape, (both, shared))
        return tuple(coeffs)

    coeffs, given, column = lax.cond(first_of_pair, gathering, levels_early)
    handed = lax.ppermute(given, "bx", [(i, i ^ 1) for i in range(0, lax.axis_size("bx"), 2)])
    both = lax.cond(
        first_of_pair,
        lambda: jnp.stack([coeffs, coeffs]),
        lambda: pair_gather(coeffs, *levels[packing.split]),
    )

    def near_only():
        near = near_of(packing, 0, given, shared, (column,), own_blocks, own_index)
        return near, coeffs[0], coeffs[1]

    def levels_late():
        gathered = both
        for level in range(packing.split, len(levels)):
            kernel = functools.partial(next_level, packing, level, levels[level])
            shape = coeffs_shape
            if level == len(levels) - 1:
                kernel = functools.partial(last_level, packing, level, levels[level])
                shape = (pltpu.VMEM((excite, rank), jnp.bfloat16),) * 2
            result = in_vmem(kernel, f"level_{level}", shape, (gathered, handed, later))
            if level < len(levels) - 1:
                gathered = pair_gather(result, *levels[level + 1])
        beside, result = lax.optimization_barrier((handed, tuple(result)))
        near = near_of(packing, 1, beside, shared, (), own_blocks, own_index)
        return near, *result

    near, final_given, final = lax.cond(first_of_pair, near_only, levels_late)
    taken = pair_gather(final_given, "bx", 0)
    return response_of(taken, final, near, far_expand[0, 0])


def solution(mesh):
    placed = (
        P(None, "bx", "by", None),
        P("bx", "by", None, None, None, None),
        P("bx", "by", None, None),
        P("bx", "by", None, None),
        P("bx", "by", None, None, None, None),
        P("bx", "by", None, None),
    )
    return jax.shard_map(
        per_device, mesh=mesh, in_specs=placed, out_specs=P(None, "bx", "by", None), check_vma=False
    )
```

```python
import functools

import jax
import jax.numpy as jnp
from jax import lax
from jax.experimental import pallas as pl
from jax.experimental.pallas import tpu as pltpu
from jax.sharding import PartitionSpec as P

BOTH = ("bx", "by")
LANES = 128
GRANT = pltpu.CompilerParams(vmem_limit_bytes=8 << 20)


def pair_gather(values, axis, apart):
    count = lax.axis_size(axis)
    pairs = [[i, i ^ 1 << apart] for i in range(count) if not i >> apart & 1]
    return lax.all_gather(values, axis, axis_index_groups=pairs)


def four_exchange(copies, axis, apart):
    groups = []
    for base in range(lax.axis_size(axis)):
        if not base >> apart & 3:
            groups.append([base | g << apart for g in range(4)])
    return lax.all_to_all(copies, axis, 0, 0, axis_index_groups=groups)


def swapped(values, axis, phase):
    count_x, count_y = lax.axis_size("bx"), lax.axis_size("by")
    moves = []
    for x in range(0, count_x, 2):
        for y in range(count_y):
            place, count = (x // 2, count_x // 2) if axis == "bx" else (y, count_y)
            other = place + (1 if place % 2 == phase else -1)
            if 0 <= other < count:
                target = 2 * other * count_y + y if axis == "bx" else x * count_y + other
                moves.append((x * count_y + y, target))
    return lax.ppermute(values, BOTH, moves)


def fetched_from(values, apart):
    count_x, count_y = lax.axis_size("bx"), lax.axis_size("by")
    at = [x * count_y + y for x in range(0, count_x, 2) for y in range(count_y)]
    return lax.ppermute(values, BOTH, [(i, i ^ 1 << apart) for i in at])


def surroundings(boxes):
    even = lax.axis_index("bx") >> 1 & 1 == 0
    first = swapped(jnp.where(even, boxes[1], boxes[0]), "bx", 0)
    second = swapped(jnp.where(even, boxes[0], boxes[1]), "bx", 1)
    before, after = jnp.where(even, second, first), jnp.where(even, first, second)
    row = jnp.concatenate([before[None], boxes, after[None]])
    even = lax.axis_index("by") & 1 == 0
    first, second = swapped(row, "by", 0), swapped(row, "by", 1)
    return jnp.where(even, second, first), row, jnp.where(even, first, second)


class Packing:
    def __init__(self, levels, rank, excite, unknowns):
        self.excite, self.blocks = excite, unknowns // LANES
        self.split = levels - 3
        self.level_rows = 2 * rank
        self.box_rows = self.blocks * excite
        self.coeffs = self.split * self.level_rows
        self.sources = self.coeffs + excite
        self.first_rows = self.sources + self.box_rows
        self.late_rows = (levels - self.split) * self.level_rows
        self.late = 7 * self.box_rows
        self.fetched = self.late + self.late_rows
        self.second_rows = self.fetched + 2 * self.level_rows

    def place_of(self, level):
        return (level if level < self.split else level - self.split) * self.level_rows


def pack(packing, mixing_hbm, sources_hbm, project_hbm, packed, later, sources, project, sems):
    excite = packing.excite
    wide = [
        pltpu.make_async_copy(sources_hbm, sources, sems.at[0]),
        pltpu.make_async_copy(project_hbm, project, sems.at[1]),
    ]
    for copy in wide:
        copy.start()
    rest = [
        pltpu.make_async_copy(
            mixing_hbm.at[pl.ds(0, packing.coeffs)],
            packed.at[pl.ds(0, packing.coeffs)],
            sems.at[2],
        ),
        pltpu.make_async_copy(
            mixing_hbm.at[pl.ds(packing.coeffs, packing.late_rows)], later, sems.at[3]
        ),
    ]
    for block in range(packing.blocks):
        rest.append(
            pltpu.make_async_copy(
                sources_hbm.at[:, pl.ds(block * LANES, LANES)],
                packed.at[pl.ds(packing.sources + block * excite, excite)],
                sems.at[4 + block],
            )
        )
    for copy in rest:
        copy.start()
    for copy in wide:
        copy.wait()
    packed[pl.ds(packing.coeffs, excite)] = jnp.dot(
        sources[...], project[...], preferred_element_type=jnp.float32
    ).astype(jnp.bfloat16)
    for copy in rest:
        copy.wait()


def packed_own(packing, mixing, sources, project):
    vmem = pl.BlockSpec(memory_space=pltpu.VMEM)
    operands = (mixing.reshape(-1, LANES), sources, project)
    return pl.pallas_call(
        functools.partial(pack, packing),
        name="pack",
        compiler_params=GRANT,
        out_shape=tuple(
            pltpu.VMEM((rows, LANES), jnp.bfloat16)
            for rows in (packing.first_rows, packing.late_rows)
        ),
        in_specs=[pl.BlockSpec(memory_space=pl.ANY)] * 3,
        out_specs=(vmem, vmem),
        scratch_shapes=[
            pltpu.VMEM(sources.shape, sources.dtype),
            pltpu.VMEM(project.shape, project.dtype),
            pltpu.SemaphoreType.DMA((4 + packing.blocks,)),
        ],
    )(*(pltpu.with_memory_space_constraint(x, pltpu.HBM) for x in operands))


def first_level(packing, early, coeffs):
    given = [early[box, pl.ds(packing.coeffs, packing.excite)] for box in range(2)]
    for box in range(2):
        pair = jnp.concatenate([given[box], given[1 - box]], axis=1)
        coeffs[box] = jnp.dot(
            pair, early[box, pl.ds(0, packing.level_rows)], preferred_element_type=jnp.float32
        ).astype(coeffs.dtype)


def mixed(packing, level, place, both, blocks):
    axis, apart = place
    upper = lax.axis_index(axis) >> apart & 1
    if level < packing.split:
        blocks = [blocks[0].at[box] for box in range(2)]
        starts = [packing.place_of(level)] * 2
    else:
        starts = [packing.late + packing.place_of(level), packing.place_of(level)]
    sums = []
    for box in range(2):
        pair = jnp.concatenate([both[upper, box], both[1 - upper, box]], axis=1)
        weights = blocks[box][pl.ds(starts[box], packing.level_rows)]
        sums.append(
            jnp.dot(pair, weights, preferred_element_type=jnp.float32).astype(jnp.bfloat16)
        )
    return sums


def two_levels(packing, level, place, four, shared, theirs, own, coeffs):
    axis, apart = place
    rows = packing.level_rows
    bit, next_bit = (lax.axis_index(axis) >> apart + n & 1 for n in range(2))
    start = packing.place_of(level)

    def product(low, high, weights):
        pair = jnp.concatenate([low, high], axis=1)
        return jnp.dot(pair, weights, preferred_element_type=jnp.float32).astype(jnp.bfloat16)

    for box in range(2):
        near, far = 2 * next_bit, 2 * (1 - next_bit)
        here = product(
            four[near + bit, box], four[near + 1 - bit, box], shared[box, pl.ds(start, rows)]
        )
        there = product(
            four[far + bit, box],
            four[far + 1 - bit, box],
            theirs[pl.ds(packing.fetched + box * rows, rows)],
        )
        at = packing.place_of(level + 1)
        weights = theirs[pl.ds(packing.late + at, rows)] if box == 0 else own[pl.ds(at, rows)]
        coeffs[box] = product(here, there, weights)


def spread_level(packing, level, place, both, *rest):
    for box, value in enumerate(mixed(packing, level, place, both, rest[:1])):
        for member in range(4):
            rest[1][member, box] = value


def next_level(packing, level, place, both, *rest):
    blocks = rest[: 1 if level < packing.split else 2]
    coeffs = rest[len(blocks)]
    for box, value in enumerate(mixed(packing, level, place, both, blocks)):
        coeffs[box] = value


def last_level(packing, level, place, both, theirs, own, given, final):
    given[...], final[...] = mixed(packing, level, place, both, (theirs, own))


def in_vmem(kernel, name, out_shape, operands):
    vmem = pl.BlockSpec(memory_space=pltpu.VMEM)
    call = pl.pallas_call(
        kernel,
        name=name,
        compiler_params=GRANT,
        out_shape=out_shape,
        in_specs=[vmem] * len(operands),
        out_specs=jax.tree.map(lambda _: vmem, out_shape),
    )
    return call(*(pltpu.with_memory_space_constraint(x, pltpu.VMEM) for x in operands))


def near_field(
    packing, offset, beside, shared, *rest
):
    column, (near_blocks, index_ref, near, index, sem) = rest[:-5], rest[-5:]
    excite, rows = packing.excite, packing.box_rows
    targets, positions = index.shape
    block_len = near_blocks.shape[1]
    indices = pltpu.make_async_copy(index_ref, index, sem)
    indices.start()
    indices.wait()

    def block_at(x, y, block):
        at = pl.multiple_of(block * excite, excite)
        if x == 0:
            return column[0][pl.ds(y * rows + at, excite)]
        if y == 1 and x < 3:
            return shared[x - 1, pl.ds(packing.sources + at, excite)]
        return beside[pl.ds((3 if y == 1 else x - 1 + 2 * y) * rows + at, excite)]

    for target in range(targets):
        picked, blocks = [], []
        for position in range(positions):
            x, y = position // 3 + offset, position % 3
            picked.append(block_at(x, y, index[target, position]))
            start = (target * positions + position) * block_len
            blocks.append(near_blocks[pl.ds(start, block_len)])
        near[:, pl.ds(target * block_len, block_len)] = lax.dot_general(
            jnp.concatenate(picked, axis=1),
            jnp.concatenate(blocks, axis=1),
            (((1,), (1,)), ((), ())),
            preferred_element_type=jnp.float32,
        )


def near_of(packing, offset, beside, shared, column, near_blocks, near_index):
    vmem = pl.BlockSpec(memory_space=pltpu.VMEM)
    around = (beside, shared, *column)
    operands = [pltpu.with_memory_space_constraint(x, pltpu.VMEM) for x in around]
    operands += [near_blocks.reshape(-1, near_blocks.shape[3]), near_index]
    return pl.pallas_call(
        functools.partial(near_field, packing, offset),
        name=f"near_{offset}",
        compiler_params=GRANT,
        out_shape=pltpu.VMEM((packing.excite, packing.blocks * LANES), jnp.float32),
        in_specs=[vmem] * len(operands),
        out_specs=vmem,
        scratch_shapes=[
            pltpu.SMEM(near_index.shape, near_index.dtype),
            pltpu.SemaphoreType.DMA,
        ],
    )(*operands)


def respond(taken, own_final, near, far_expand, response_hbm, response, sems):
    first_of_pair = lax.axis_index("bx") & 1 == 0
    final = jnp.where(first_of_pair, taken[1], own_final[...])
    width = response.shape[3] // sems.shape[0]
    copies = []
    for part in range(sems.shape[0]):
        lanes = pl.ds(part * width, width)
        response[:, 0, 0, lanes] = near[:, lanes] + jnp.dot(
            final, far_expand[:, lanes], preferred_element_type=jnp.float32
        )
        ends = response.at[:, :, :, lanes], response_hbm.at[:, :, :, lanes]
        copies.append(pltpu.make_async_copy(*ends, sems.at[part]))
        copies[-1].start()
    for copy in copies:
        copy.wait()


def response_of(taken, final, near, far_expand):
    vmem = pl.BlockSpec(memory_space=pltpu.VMEM)
    shape = (near.shape[0], 1, 1, near.shape[1])
    held = [pltpu.with_memory_space_constraint(x, pltpu.VMEM) for x in (taken, final, near)]
    return pl.pallas_call(
        respond,
        name="respond",
        compiler_params=GRANT,
        out_shape=jax.ShapeDtypeStruct(shape, jnp.float32),
        in_specs=[vmem] * 4,
        out_specs=pl.BlockSpec(memory_space=pl.ANY),
        scratch_shapes=[pltpu.VMEM(shape, jnp.float32), pltpu.SemaphoreType.DMA((4,))],
    )(*held, far_expand)


def per_device(sources, near_blocks, near_index, far_project, far_mixing, far_expand):
    own_sources, own_blocks, own_index = sources[:, 0, 0], near_blocks[0, 0], near_index[0, 0]
    excite, unknowns = own_sources.shape
    rank = far_project.shape[3]
    first_of_pair = lax.axis_index("bx") & 1 == 0
    levels = [("bx", n) for n in range(lax.axis_size("bx").bit_length() - 1)]
    levels += [("by", n) for n in range(lax.axis_size("by").bit_length() - 1)]
    packing = Packing(len(levels), rank, excite, unknowns)
    packed, later = packed_own(packing, far_mixing[0, 0], own_sources, far_project[0, 0])
    shared = pair_gather(packed, "bx", 0)
    coeffs_shape = pltpu.VMEM((2, excite, rank), jnp.bfloat16)
    four_shape = pltpu.VMEM((4, 2, excite, rank), jnp.bfloat16)
    column_shape = pltpu.VMEM((3 * packing.box_rows, LANES), jnp.bfloat16)
    given_shape = pltpu.VMEM((packing.second_rows, LANES), jnp.bfloat16)
    merged = packing.split - 1
    apart = levels[merged][1]

    def gathering():
        start = packing.place_of(merged)
        fetched = fetched_from(shared[:, start : start + packing.level_rows], apart + 1)
        boxes = shared[:, packing.sources :].reshape(2, packing.blocks, excite, LANES)
        below, row, above = surroundings(boxes)
        given = jnp.concatenate([below[1:], row[3:], above[1:]]).reshape(-1, LANES)
        column = jnp.stack([below[0], row[0], above[0]]).reshape(-1, LANES)
        given = jnp.concatenate([given, later, fetched.reshape(-1, LANES)])
        return jnp.zeros((4, 2, excite, rank), jnp.bfloat16), given, column

    def levels_early():
        coeffs = in_vmem(functools.partial(first_level, packing), "level_0", coeffs_shape, (shared,))
        for level in range(1, merged):
            kernel, shape = next_level, coeffs_shape
            if level == merged - 1:
                kernel, shape = spread_level, (four_shape, given_shape, column_shape)
            both = pair_gather(coeffs, *levels[level])
            kernel = functools.partial(kernel, packing, level, levels[level])
            coeffs = in_vmem(kernel, f"level_{level}", shape, (both, shared))
        return tuple(coeffs)

    copies, given, column = lax.cond(first_of_pair, gathering, levels_early)
    handed = lax.ppermute(given, "bx", [(i, i ^ 1) for i in range(0, lax.axis_size("bx"), 2)])
    four = lax.cond(
        first_of_pair, lambda: copies, lambda: four_exchange(copies, *levels[merged])
    )

    def near_only():
        near = near_of(packing, 0, given, shared, (column,), own_blocks, own_index)
        return near, copies[0, 0], copies[0, 1]

    def levels_late():
        kernel = functools.partial(two_levels, packing, merged, levels[merged])
        result = in_vmem(kernel, "two_levels", coeffs_shape, (four, shared, handed, later))
        for level in range(merged + 2, len(levels)):
            kernel = functools.partial(next_level, packing, level, levels[level])
            shape = coeffs_shape
            if level == len(levels) - 1:
                kernel = functools.partial(last_level, packing, level, levels[level])
                shape = (pltpu.VMEM((excite, rank), jnp.bfloat16),) * 2
            both = pair_gather(result, *levels[level])
            result = in_vmem(kernel, f"level_{level}", shape, (both, handed, later))
        beside, result = lax.optimization_barrier((handed, tuple(result)))
        near = near_of(packing, 1, beside, shared, (), own_blocks, own_index)
        return near, *result

    near, final_given, final = lax.cond(first_of_pair, near_only, levels_late)
    taken = pair_gather(final_given, "bx", 0)
    return response_of(taken, final, near, far_expand[0, 0])


def solution(mesh):
    placed = (
        P(None, "bx", "by", None),
        P("bx", "by", None, None, None, None),
        P("bx", "by", None, None),
        P("bx", "by", None, None),
        P("bx", "by", None, None, None, None),
        P("bx", "by", None, None),
    )
    return jax.shard_map(
        per_device, mesh=mesh, in_specs=placed, out_specs=P(None, "bx", "by", None), check_vma=False
    )
```

```python
import functools

import jax
import jax.numpy as jnp
from jax import lax
from jax.experimental import pallas as pl
from jax.experimental.pallas import tpu as pltpu
from jax.sharding import PartitionSpec as P

BOTH = ("bx", "by")
LANES = 128
GRANT = pltpu.CompilerParams(vmem_limit_bytes=8 << 20)


def pair_gather(values, axis, apart):
    count = lax.axis_size(axis)
    pairs = [[i, i ^ 1 << apart] for i in range(count) if not i >> apart & 1]
    return lax.all_gather(values, axis, axis_index_groups=pairs)


def four_exchange(copies, axis, apart):
    groups = []
    for base in range(lax.axis_size(axis)):
        if not base >> apart & 3:
            groups.append([base | g << apart for g in range(4)])
    return lax.all_to_all(copies, axis, 0, 0, axis_index_groups=groups)


def swapped(values, axis, phase):
    count_x, count_y = lax.axis_size("bx"), lax.axis_size("by")
    moves = []
    for x in range(0, count_x, 2):
        for y in range(count_y):
            place, count = (x // 2, count_x // 2) if axis == "bx" else (y, count_y)
            other = place + (1 if place % 2 == phase else -1)
            if 0 <= other < count:
                target = 2 * other * count_y + y if axis == "bx" else x * count_y + other
                moves.append((x * count_y + y, target))
    return lax.ppermute(values, BOTH, moves)


def fetched_from(values, apart):
    count_x, count_y = lax.axis_size("bx"), lax.axis_size("by")
    at = [x * count_y + y for x in range(0, count_x, 2) for y in range(count_y)]
    return lax.ppermute(values, BOTH, [(i, i ^ 1 << apart) for i in at])


def surroundings(boxes, meanwhile):
    even = lax.axis_index("bx") >> 1 & 1 == 0
    first = swapped(jnp.where(even, boxes[1], boxes[0]), "bx", 0)
    second = swapped(jnp.where(even, boxes[0], boxes[1]), "bx", 1)
    before, after = jnp.where(even, second, first), jnp.where(even, first, second)
    row = jnp.concatenate([before[None], boxes, after[None]])
    row, meanwhile = lax.optimization_barrier((row, meanwhile))
    even = lax.axis_index("by") & 1 == 0
    first, second = swapped(row, "by", 0), swapped(row, "by", 1)
    return jnp.where(even, second, first), row, jnp.where(even, first, second), meanwhile


class Packing:
    def __init__(self, levels, rank, excite, unknowns):
        self.excite, self.blocks = excite, unknowns // LANES
        self.split = levels - 3
        self.level_rows = 2 * rank
        self.box_rows = self.blocks * excite
        self.coeffs = self.split * self.level_rows
        self.sources = self.coeffs + excite
        self.first_rows = self.sources + self.box_rows
        self.late_rows = (levels - self.split) * self.level_rows
        self.late = 7 * self.box_rows
        self.fetched = self.late + self.late_rows
        self.second_rows = self.fetched + 2 * self.level_rows

    def place_of(self, level):
        return (level if level < self.split else level - self.split) * self.level_rows


def pack(packing, mixing_hbm, sources_hbm, project_hbm, packed, later, sources, project, sems):
    excite = packing.excite
    wide = [
        pltpu.make_async_copy(sources_hbm, sources, sems.at[0]),
        pltpu.make_async_copy(project_hbm, project, sems.at[1]),
    ]
    for copy in wide:
        copy.start()
    rest = [
        pltpu.make_async_copy(
            mixing_hbm.at[pl.ds(0, packing.coeffs)],
            packed.at[pl.ds(0, packing.coeffs)],
            sems.at[2],
        ),
        pltpu.make_async_copy(
            mixing_hbm.at[pl.ds(packing.coeffs, packing.late_rows)], later, sems.at[3]
        ),
    ]
    for block in range(packing.blocks):
        rest.append(
            pltpu.make_async_copy(
                sources_hbm.at[:, pl.ds(block * LANES, LANES)],
                packed.at[pl.ds(packing.sources + block * excite, excite)],
                sems.at[4 + block],
            )
        )
    for copy in rest:
        copy.start()
    for copy in wide:
        copy.wait()
    packed[pl.ds(packing.coeffs, excite)] = jnp.dot(
        sources[...], project[...], preferred_element_type=jnp.float32
    ).astype(jnp.bfloat16)
    for copy in rest:
        copy.wait()


def packed_own(packing, mixing, sources, project):
    vmem = pl.BlockSpec(memory_space=pltpu.VMEM)
    operands = (mixing.reshape(-1, LANES), sources, project)
    return pl.pallas_call(
        functools.partial(pack, packing),
        name="pack",
        compiler_params=GRANT,
        out_shape=tuple(
            pltpu.VMEM((rows, LANES), jnp.bfloat16)
            for rows in (packing.first_rows, packing.late_rows)
        ),
        in_specs=[pl.BlockSpec(memory_space=pl.ANY)] * 3,
        out_specs=(vmem, vmem),
        scratch_shapes=[
            pltpu.VMEM(sources.shape, sources.dtype),
            pltpu.VMEM(project.shape, project.dtype),
            pltpu.SemaphoreType.DMA((4 + packing.blocks,)),
        ],
    )(*(pltpu.with_memory_space_constraint(x, pltpu.HBM) for x in operands))


def first_level(packing, early, coeffs):
    given = [early[box, pl.ds(packing.coeffs, packing.excite)] for box in range(2)]
    for box in range(2):
        pair = jnp.concatenate([given[box], given[1 - box]], axis=1)
        coeffs[box] = jnp.dot(
            pair, early[box, pl.ds(0, packing.level_rows)], preferred_element_type=jnp.float32
        ).astype(coeffs.dtype)


def mixed(packing, level, place, both, blocks):
    axis, apart = place
    upper = lax.axis_index(axis) >> apart & 1
    if level < packing.split:
        blocks = [blocks[0].at[box] for box in range(2)]
        starts = [packing.place_of(level)] * 2
    else:
        starts = [packing.late + packing.place_of(level), packing.place_of(level)]
    sums = []
    for box in range(2):
        pair = jnp.concatenate([both[upper, box], both[1 - upper, box]], axis=1)
        weights = blocks[box][pl.ds(starts[box], packing.level_rows)]
        sums.append(
            jnp.dot(pair, weights, preferred_element_type=jnp.float32).astype(jnp.bfloat16)
        )
    return sums


def two_levels(packing, level, place, four, shared, theirs, own, coeffs):
    axis, apart = place
    rows = packing.level_rows
    bit, next_bit = (lax.axis_index(axis) >> apart + n & 1 for n in range(2))
    start = packing.place_of(level)

    def product(low, high, weights):
        pair = jnp.concatenate([low, high], axis=1)
        return jnp.dot(pair, weights, preferred_element_type=jnp.float32).astype(jnp.bfloat16)

    for box in range(2):
        near, far = 2 * next_bit, 2 * (1 - next_bit)
        here = product(
            four[near + bit, box], four[near + 1 - bit, box], shared[box, pl.ds(start, rows)]
        )
        there = product(
            four[far + bit, box],
            four[far + 1 - bit, box],
            theirs[pl.ds(packing.fetched + box * rows, rows)],
        )
        at = packing.place_of(level + 1)
        weights = theirs[pl.ds(packing.late + at, rows)] if box == 0 else own[pl.ds(at, rows)]
        coeffs[box] = product(here, there, weights)


def spread_level(packing, level, place, both, *rest):
    for box, value in enumerate(mixed(packing, level, place, both, rest[:1])):
        for member in range(4):
            rest[1][member, box] = value


def next_level(packing, level, place, both, *rest):
    blocks = rest[: 1 if level < packing.split else 2]
    coeffs = rest[len(blocks)]
    for box, value in enumerate(mixed(packing, level, place, both, blocks)):
        coeffs[box] = value


def last_level(packing, level, place, both, theirs, own, given, final):
    given[...], final[...] = mixed(packing, level, place, both, (theirs, own))


def in_vmem(kernel, name, out_shape, operands):
    vmem = pl.BlockSpec(memory_space=pltpu.VMEM)
    call = pl.pallas_call(
        kernel,
        name=name,
        compiler_params=GRANT,
        out_shape=out_shape,
        in_specs=[vmem] * len(operands),
        out_specs=jax.tree.map(lambda _: vmem, out_shape),
    )
    return call(*(pltpu.with_memory_space_constraint(x, pltpu.VMEM) for x in operands))


def near_field(
    packing, offset, beside, shared, *rest
):
    column, (near_blocks, index_ref, near, index, sem) = rest[:-5], rest[-5:]
    excite, rows = packing.excite, packing.box_rows
    targets, positions = index.shape
    block_len = near_blocks.shape[1]
    indices = pltpu.make_async_copy(index_ref, index, sem)
    indices.start()
    indices.wait()

    def block_at(x, y, block):
        at = pl.multiple_of(block * excite, excite)
        if x == 0:
            return column[0][pl.ds(y * rows + at, excite)]
        if y == 1 and x < 3:
            return shared[x - 1, pl.ds(packing.sources + at, excite)]
        return beside[pl.ds((3 if y == 1 else x - 1 + 2 * y) * rows + at, excite)]

    for target in range(targets):
        picked, blocks = [], []
        for position in range(positions):
            x, y = position // 3 + offset, position % 3
            picked.append(block_at(x, y, index[target, position]))
            start = (target * positions + position) * block_len
            blocks.append(near_blocks[pl.ds(start, block_len)])
        near[:, pl.ds(target * block_len, block_len)] = lax.dot_general(
            jnp.concatenate(picked, axis=1),
            jnp.concatenate(blocks, axis=1),
            (((1,), (1,)), ((), ())),
            preferred_element_type=jnp.float32,
        )


def near_of(packing, offset, beside, shared, column, near_blocks, near_index):
    vmem = pl.BlockSpec(memory_space=pltpu.VMEM)
    around = (beside, shared, *column)
    operands = [pltpu.with_memory_space_constraint(x, pltpu.VMEM) for x in around]
    operands += [near_blocks.reshape(-1, near_blocks.shape[3]), near_index]
    return pl.pallas_call(
        functools.partial(near_field, packing, offset),
        name=f"near_{offset}",
        compiler_params=GRANT,
        out_shape=pltpu.VMEM((packing.excite, packing.blocks * LANES), jnp.float32),
        in_specs=[vmem] * len(operands),
        out_specs=vmem,
        scratch_shapes=[
            pltpu.SMEM(near_index.shape, near_index.dtype),
            pltpu.SemaphoreType.DMA,
        ],
    )(*operands)


def respond(taken, own_final, near, far_expand, response_hbm, response, sems):
    first_of_pair = lax.axis_index("bx") & 1 == 0
    final = jnp.where(first_of_pair, taken[1], own_final[...])
    width = response.shape[3] // sems.shape[0]
    copies = []
    for part in range(sems.shape[0]):
        lanes = pl.ds(part * width, width)
        response[:, 0, 0, lanes] = near[:, lanes] + jnp.dot(
            final, far_expand[:, lanes], preferred_element_type=jnp.float32
        )
        ends = response.at[:, :, :, lanes], response_hbm.at[:, :, :, lanes]
        copies.append(pltpu.make_async_copy(*ends, sems.at[part]))
        copies[-1].start()
    for copy in copies:
        copy.wait()


def response_of(taken, final, near, far_expand):
    vmem = pl.BlockSpec(memory_space=pltpu.VMEM)
    shape = (near.shape[0], 1, 1, near.shape[1])
    held = [pltpu.with_memory_space_constraint(x, pltpu.VMEM) for x in (taken, final, near)]
    return pl.pallas_call(
        respond,
        name="respond",
        compiler_params=GRANT,
        out_shape=jax.ShapeDtypeStruct(shape, jnp.float32),
        in_specs=[vmem] * 4,
        out_specs=pl.BlockSpec(memory_space=pl.ANY),
        scratch_shapes=[pltpu.VMEM(shape, jnp.float32), pltpu.SemaphoreType.DMA((4,))],
    )(*held, far_expand)


def per_device(sources, near_blocks, near_index, far_project, far_mixing, far_expand):
    own_sources, own_blocks, own_index = sources[:, 0, 0], near_blocks[0, 0], near_index[0, 0]
    excite, unknowns = own_sources.shape
    rank = far_project.shape[3]
    first_of_pair = lax.axis_index("bx") & 1 == 0
    levels = [("bx", n) for n in range(lax.axis_size("bx").bit_length() - 1)]
    levels += [("by", n) for n in range(lax.axis_size("by").bit_length() - 1)]
    packing = Packing(len(levels), rank, excite, unknowns)
    packed, later = packed_own(packing, far_mixing[0, 0], own_sources, far_project[0, 0])
    shared = pair_gather(packed, "bx", 0)
    coeffs_shape = pltpu.VMEM((2, excite, rank), jnp.bfloat16)
    four_shape = pltpu.VMEM((4, 2, excite, rank), jnp.bfloat16)
    column_shape = pltpu.VMEM((3 * packing.box_rows, LANES), jnp.bfloat16)
    given_shape = pltpu.VMEM((packing.second_rows, LANES), jnp.bfloat16)
    merged = packing.split - 1
    apart = levels[merged][1]

    def gathering():
        start = packing.place_of(merged)
        fetched = fetched_from(shared[:, start : start + packing.level_rows], apart + 1)
        boxes = shared[:, packing.sources :].reshape(2, packing.blocks, excite, LANES)
        below, row, above, fetched = surroundings(boxes, fetched)
        given = jnp.concatenate([below[1:], row[3:], above[1:]]).reshape(-1, LANES)
        column = jnp.stack([below[0], row[0], above[0]]).reshape(-1, LANES)
        given = jnp.concatenate([given, later, fetched.reshape(-1, LANES)])
        return jnp.zeros((4, 2, excite, rank), jnp.bfloat16), given, column

    def levels_early():
        coeffs = in_vmem(functools.partial(first_level, packing), "level_0", coeffs_shape, (shared,))
        for level in range(1, merged):
            kernel, shape = next_level, coeffs_shape
            if level == merged - 1:
                kernel, shape = spread_level, (four_shape, given_shape, column_shape)
            both = pair_gather(coeffs, *levels[level])
            kernel = functools.partial(kernel, packing, level, levels[level])
            coeffs = in_vmem(kernel, f"level_{level}", shape, (both, shared))
        return tuple(coeffs)

    copies, given, column = lax.cond(first_of_pair, gathering, levels_early)
    handed = lax.ppermute(given, "bx", [(i, i ^ 1) for i in range(0, lax.axis_size("bx"), 2)])
    four = lax.cond(
        first_of_pair, lambda: copies, lambda: four_exchange(copies, *levels[merged])
    )

    def near_only():
        near = near_of(packing, 0, given, shared, (column,), own_blocks, own_index)
        return near, copies[0, 0], copies[0, 1]

    def levels_late():
        kernel = functools.partial(two_levels, packing, merged, levels[merged])
        result = in_vmem(kernel, "two_levels", coeffs_shape, (four, shared, handed, later))
        for level in range(merged + 2, len(levels)):
            kernel = functools.partial(next_level, packing, level, levels[level])
            shape = coeffs_shape
            if level == len(levels) - 1:
                kernel = functools.partial(last_level, packing, level, levels[level])
                shape = (pltpu.VMEM((excite, rank), jnp.bfloat16),) * 2
            both = pair_gather(result, *levels[level])
            result = in_vmem(kernel, f"level_{level}", shape, (both, handed, later))
        beside, result = lax.optimization_barrier((handed, tuple(result)))
        near = near_of(packing, 1, beside, shared, (), own_blocks, own_index)
        return near, *result

    near, final_given, final = lax.cond(first_of_pair, near_only, levels_late)
    taken = pair_gather(final_given, "bx", 0)
    return response_of(taken, final, near, far_expand[0, 0])


def solution(mesh):
    placed = (
        P(None, "bx", "by", None),
        P("bx", "by", None, None, None, None),
        P("bx", "by", None, None),
        P("bx", "by", None, None),
        P("bx", "by", None, None, None, None),
        P("bx", "by", None, None),
    )
    return jax.shard_map(
        per_device, mesh=mesh, in_specs=placed, out_specs=P(None, "bx", "by", None), check_vma=False
    )
```

```python
import functools

import jax
import jax.numpy as jnp
from jax import lax
from jax.experimental import pallas as pl
from jax.experimental.pallas import tpu as pltpu
from jax.sharding import PartitionSpec as P

BOTH = ("bx", "by")
LANES = 128
GRANT = pltpu.CompilerParams(vmem_limit_bytes=8 << 20)


def pair_gather(values, axis, apart):
    count = lax.axis_size(axis)
    pairs = [[i, i ^ 1 << apart] for i in range(count) if not i >> apart & 1]
    return lax.all_gather(values, axis, axis_index_groups=pairs)


def four_exchange(copies, axis, apart):
    groups = []
    for base in range(lax.axis_size(axis)):
        if not base >> apart & 3:
            groups.append([base | g << apart for g in range(4)])
    return lax.all_to_all(copies, axis, 0, 0, axis_index_groups=groups)


def swapped(values, axis, phase):
    count_x, count_y = lax.axis_size("bx"), lax.axis_size("by")
    moves = []
    for x in range(0, count_x, 2):
        for y in range(count_y):
            place, count = (x // 2, count_x // 2) if axis == "bx" else (y, count_y)
            other = place + (1 if place % 2 == phase else -1)
            if 0 <= other < count:
                target = 2 * other * count_y + y if axis == "bx" else x * count_y + other
                moves.append((x * count_y + y, target))
    return lax.ppermute(values, BOTH, moves)


def fetched_from(values, apart):
    count_x, count_y = lax.axis_size("bx"), lax.axis_size("by")
    at = [x * count_y + y for x in range(0, count_x, 2) for y in range(count_y)]
    return lax.ppermute(values, BOTH, [(i, i ^ 1 << apart) for i in at])


def surroundings(boxes, meanwhile):
    even = lax.axis_index("bx") >> 1 & 1 == 0
    second = swapped(jnp.where(even, boxes[0], boxes[1]), "bx", 1)
    first = swapped(jnp.where(even, boxes[1], boxes[0]), "bx", 0)
    before, after = jnp.where(even, second, first), jnp.where(even, first, second)
    row = jnp.concatenate([before[None], boxes, after[None]])
    even = lax.axis_index("by") & 1 == 0
    first = swapped(row, "by", 0)
    row, meanwhile = lax.optimization_barrier((row, meanwhile))
    second = swapped(row, "by", 1)
    return jnp.where(even, second, first), row, jnp.where(even, first, second), meanwhile


class Packing:
    def __init__(self, levels, rank, excite, unknowns):
        self.excite, self.blocks = excite, unknowns // LANES
        self.split = levels - 3
        self.level_rows = 2 * rank
        self.box_rows = self.blocks * excite
        self.coeffs = self.split * self.level_rows
        self.sources = self.coeffs + excite
        self.first_rows = self.sources + self.box_rows
        self.late_rows = (levels - self.split) * self.level_rows
        self.late = 7 * self.box_rows
        self.fetched = self.late + self.late_rows
        self.second_rows = self.fetched + 2 * self.level_rows

    def place_of(self, level):
        return (level if level < self.split else level - self.split) * self.level_rows


def pack(packing, mixing_hbm, sources_hbm, project_hbm, packed, later, sources, project, sems):
    excite = packing.excite
    wide = [
        pltpu.make_async_copy(sources_hbm, sources, sems.at[0]),
        pltpu.make_async_copy(project_hbm, project, sems.at[1]),
    ]
    for copy in wide:
        copy.start()
    rest = [
        pltpu.make_async_copy(
            mixing_hbm.at[pl.ds(0, packing.coeffs)],
            packed.at[pl.ds(0, packing.coeffs)],
            sems.at[2],
        ),
        pltpu.make_async_copy(
            mixing_hbm.at[pl.ds(packing.coeffs, packing.late_rows)], later, sems.at[3]
        ),
    ]
    for block in range(packing.blocks):
        rest.append(
            pltpu.make_async_copy(
                sources_hbm.at[:, pl.ds(block * LANES, LANES)],
                packed.at[pl.ds(packing.sources + block * excite, excite)],
                sems.at[4 + block],
            )
        )
    for copy in rest:
        copy.start()
    for copy in wide:
        copy.wait()
    packed[pl.ds(packing.coeffs, excite)] = jnp.dot(
        sources[...], project[...], preferred_element_type=jnp.float32
    ).astype(jnp.bfloat16)
    for copy in rest:
        copy.wait()


def packed_own(packing, mixing, sources, project):
    vmem = pl.BlockSpec(memory_space=pltpu.VMEM)
    operands = (mixing.reshape(-1, LANES), sources, project)
    return pl.pallas_call(
        functools.partial(pack, packing),
        name="pack",
        compiler_params=GRANT,
        out_shape=tuple(
            pltpu.VMEM((rows, LANES), jnp.bfloat16)
            for rows in (packing.first_rows, packing.late_rows)
        ),
        in_specs=[pl.BlockSpec(memory_space=pl.ANY)] * 3,
        out_specs=(vmem, vmem),
        scratch_shapes=[
            pltpu.VMEM(sources.shape, sources.dtype),
            pltpu.VMEM(project.shape, project.dtype),
            pltpu.SemaphoreType.DMA((4 + packing.blocks,)),
        ],
    )(*(pltpu.with_memory_space_constraint(x, pltpu.HBM) for x in operands))


def first_level(packing, early, coeffs):
    given = [early[box, pl.ds(packing.coeffs, packing.excite)] for box in range(2)]
    for box in range(2):
        pair = jnp.concatenate([given[box], given[1 - box]], axis=1)
        coeffs[box] = jnp.dot(
            pair, early[box, pl.ds(0, packing.level_rows)], preferred_element_type=jnp.float32
        ).astype(coeffs.dtype)


def mixed(packing, level, place, both, blocks):
    axis, apart = place
    upper = lax.axis_index(axis) >> apart & 1
    if level < packing.split:
        blocks = [blocks[0].at[box] for box in range(2)]
        starts = [packing.place_of(level)] * 2
    else:
        starts = [packing.late + packing.place_of(level), packing.place_of(level)]
    sums = []
    for box in range(2):
        pair = jnp.concatenate([both[upper, box], both[1 - upper, box]], axis=1)
        weights = blocks[box][pl.ds(starts[box], packing.level_rows)]
        sums.append(
            jnp.dot(pair, weights, preferred_element_type=jnp.float32).astype(jnp.bfloat16)
        )
    return sums


def two_levels(packing, level, place, four, shared, theirs, own, coeffs):
    axis, apart = place
    rows = packing.level_rows
    bit, next_bit = (lax.axis_index(axis) >> apart + n & 1 for n in range(2))
    start = packing.place_of(level)

    def product(low, high, weights):
        pair = jnp.concatenate([low, high], axis=1)
        return jnp.dot(pair, weights, preferred_element_type=jnp.float32).astype(jnp.bfloat16)

    for box in range(2):
        near, far = 2 * next_bit, 2 * (1 - next_bit)
        here = product(
            four[near + bit, box], four[near + 1 - bit, box], shared[box, pl.ds(start, rows)]
        )
        there = product(
            four[far + bit, box],
            four[far + 1 - bit, box],
            theirs[pl.ds(packing.fetched + box * rows, rows)],
        )
        at = packing.place_of(level + 1)
        weights = theirs[pl.ds(packing.late + at, rows)] if box == 0 else own[pl.ds(at, rows)]
        coeffs[box] = product(here, there, weights)


def spread_level(packing, level, place, both, *rest):
    for box, value in enumerate(mixed(packing, level, place, both, rest[:1])):
        for member in range(4):
            rest[1][member, box] = value


def next_level(packing, level, place, both, *rest):
    blocks = rest[: 1 if level < packing.split else 2]
    coeffs = rest[len(blocks)]
    for box, value in enumerate(mixed(packing, level, place, both, blocks)):
        coeffs[box] = value


def last_level(packing, level, place, both, theirs, own, given, final):
    given[...], final[...] = mixed(packing, level, place, both, (theirs, own))


def in_vmem(kernel, name, out_shape, operands):
    vmem = pl.BlockSpec(memory_space=pltpu.VMEM)
    call = pl.pallas_call(
        kernel,
        name=name,
        compiler_params=GRANT,
        out_shape=out_shape,
        in_specs=[vmem] * len(operands),
        out_specs=jax.tree.map(lambda _: vmem, out_shape),
    )
    return call(*(pltpu.with_memory_space_constraint(x, pltpu.VMEM) for x in operands))


def near_field(
    packing, offset, beside, shared, *rest
):
    column, (near_blocks, index_ref, near, index, sem) = rest[:-5], rest[-5:]
    excite, rows = packing.excite, packing.box_rows
    targets, positions = index.shape
    block_len = near_blocks.shape[1]
    indices = pltpu.make_async_copy(index_ref, index, sem)
    indices.start()
    indices.wait()

    def block_at(x, y, block):
        at = pl.multiple_of(block * excite, excite)
        if x == 0:
            return column[0][pl.ds(y * rows + at, excite)]
        if y == 1 and x < 3:
            return shared[x - 1, pl.ds(packing.sources + at, excite)]
        return beside[pl.ds((3 if y == 1 else x - 1 + 2 * y) * rows + at, excite)]

    for target in range(targets):
        picked, blocks = [], []
        for position in range(positions):
            x, y = position // 3 + offset, position % 3
            picked.append(block_at(x, y, index[target, position]))
            start = (target * positions + position) * block_len
            blocks.append(near_blocks[pl.ds(start, block_len)])
        near[:, pl.ds(target * block_len, block_len)] = lax.dot_general(
            jnp.concatenate(picked, axis=1),
            jnp.concatenate(blocks, axis=1),
            (((1,), (1,)), ((), ())),
            preferred_element_type=jnp.float32,
        )


def near_of(packing, offset, beside, shared, column, near_blocks, near_index):
    vmem = pl.BlockSpec(memory_space=pltpu.VMEM)
    around = (beside, shared, *column)
    operands = [pltpu.with_memory_space_constraint(x, pltpu.VMEM) for x in around]
    operands += [near_blocks.reshape(-1, near_blocks.shape[3]), near_index]
    return pl.pallas_call(
        functools.partial(near_field, packing, offset),
        name=f"near_{offset}",
        compiler_params=GRANT,
        out_shape=pltpu.VMEM((packing.excite, packing.blocks * LANES), jnp.float32),
        in_specs=[vmem] * len(operands),
        out_specs=vmem,
        scratch_shapes=[
            pltpu.SMEM(near_index.shape, near_index.dtype),
            pltpu.SemaphoreType.DMA,
        ],
    )(*operands)


def respond(taken, own_final, near, far_expand, response_hbm, response, sems):
    first_of_pair = lax.axis_index("bx") & 1 == 0
    final = jnp.where(first_of_pair, taken[1], own_final[...])
    width = response.shape[3] // sems.shape[0]
    copies = []
    for part in range(sems.shape[0]):
        lanes = pl.ds(part * width, width)
        response[:, 0, 0, lanes] = near[:, lanes] + jnp.dot(
            final, far_expand[:, lanes], preferred_element_type=jnp.float32
        )
        ends = response.at[:, :, :, lanes], response_hbm.at[:, :, :, lanes]
        copies.append(pltpu.make_async_copy(*ends, sems.at[part]))
        copies[-1].start()
    for copy in copies:
        copy.wait()


def response_of(taken, final, near, far_expand):
    vmem = pl.BlockSpec(memory_space=pltpu.VMEM)
    shape = (near.shape[0], 1, 1, near.shape[1])
    held = [pltpu.with_memory_space_constraint(x, pltpu.VMEM) for x in (taken, final, near)]
    return pl.pallas_call(
        respond,
        name="respond",
        compiler_params=GRANT,
        out_shape=jax.ShapeDtypeStruct(shape, jnp.float32),
        in_specs=[vmem] * 4,
        out_specs=pl.BlockSpec(memory_space=pl.ANY),
        scratch_shapes=[pltpu.VMEM(shape, jnp.float32), pltpu.SemaphoreType.DMA((4,))],
    )(*held, far_expand)


def per_device(sources, near_blocks, near_index, far_project, far_mixing, far_expand):
    own_sources, own_blocks, own_index = sources[:, 0, 0], near_blocks[0, 0], near_index[0, 0]
    excite, unknowns = own_sources.shape
    rank = far_project.shape[3]
    first_of_pair = lax.axis_index("bx") & 1 == 0
    levels = [("bx", n) for n in range(lax.axis_size("bx").bit_length() - 1)]
    levels += [("by", n) for n in range(lax.axis_size("by").bit_length() - 1)]
    packing = Packing(len(levels), rank, excite, unknowns)
    packed, later = packed_own(packing, far_mixing[0, 0], own_sources, far_project[0, 0])
    shared = pair_gather(packed, "bx", 0)
    coeffs_shape = pltpu.VMEM((2, excite, rank), jnp.bfloat16)
    four_shape = pltpu.VMEM((4, 2, excite, rank), jnp.bfloat16)
    column_shape = pltpu.VMEM((3 * packing.box_rows, LANES), jnp.bfloat16)
    given_shape = pltpu.VMEM((packing.second_rows, LANES), jnp.bfloat16)
    merged = packing.split - 1
    apart = levels[merged][1]

    def gathering():
        start = packing.place_of(merged)
        fetched = fetched_from(shared[:, start : start + packing.level_rows], apart + 1)
        boxes = shared[:, packing.sources :].reshape(2, packing.blocks, excite, LANES)
        below, row, above, fetched = surroundings(boxes, fetched)
        given = jnp.concatenate([below[1:], row[3:], above[1:]]).reshape(-1, LANES)
        column = jnp.stack([below[0], row[0], above[0]]).reshape(-1, LANES)
        given = jnp.concatenate([given, later, fetched.reshape(-1, LANES)])
        return jnp.zeros((4, 2, excite, rank), jnp.bfloat16), given, column

    def levels_early():
        coeffs = in_vmem(functools.partial(first_level, packing), "level_0", coeffs_shape, (shared,))
        for level in range(1, merged):
            kernel, shape = next_level, coeffs_shape
            if level == merged - 1:
                kernel, shape = spread_level, (four_shape, given_shape, column_shape)
            both = pair_gather(coeffs, *levels[level])
            kernel = functools.partial(kernel, packing, level, levels[level])
            coeffs = in_vmem(kernel, f"level_{level}", shape, (both, shared))
        return tuple(coeffs)

    copies, given, column = lax.cond(first_of_pair, gathering, levels_early)
    handed = lax.ppermute(given, "bx", [(i, i ^ 1) for i in range(0, lax.axis_size("bx"), 2)])
    four = lax.cond(
        first_of_pair, lambda: copies, lambda: four_exchange(copies, *levels[merged])
    )

    def near_only():
        near = near_of(packing, 0, given, shared, (column,), own_blocks, own_index)
        return near, copies[0, 0], copies[0, 1]

    def levels_late():
        kernel = functools.partial(two_levels, packing, merged, levels[merged])
        result = in_vmem(kernel, "two_levels", coeffs_shape, (four, shared, handed, later))
        for level in range(merged + 2, len(levels)):
            kernel = functools.partial(next_level, packing, level, levels[level])
            shape = coeffs_shape
            if level == len(levels) - 1:
                kernel = functools.partial(last_level, packing, level, levels[level])
                shape = (pltpu.VMEM((excite, rank), jnp.bfloat16),) * 2
            both = pair_gather(result, *levels[level])
            result = in_vmem(kernel, f"level_{level}", shape, (both, handed, later))
        beside, result = lax.optimization_barrier((handed, tuple(result)))
        near = near_of(packing, 1, beside, shared, (), own_blocks, own_index)
        return near, *result

    near, final_given, final = lax.cond(first_of_pair, near_only, levels_late)
    taken = pair_gather(final_given, "bx", 0)
    return response_of(taken, final, near, far_expand[0, 0])


def solution(mesh):
    placed = (
        P(None, "bx", "by", None),
        P("bx", "by", None, None, None, None),
        P("bx", "by", None, None),
        P("bx", "by", None, None),
        P("bx", "by", None, None, None, None),
        P("bx", "by", None, None),
    )
    return jax.shard_map(
        per_device, mesh=mesh, in_specs=placed, out_specs=P(None, "bx", "by", None), check_vma=False
    )
```

```python
import functools

import jax
import jax.numpy as jnp
from jax import lax
from jax.experimental import pallas as pl
from jax.experimental.pallas import tpu as pltpu
from jax.sharding import PartitionSpec as P


BOTH = ("bx", "by")
LANES = 128
GRANT = pltpu.CompilerParams(vmem_limit_bytes=8 << 20)


def pair_gather(values, axis, apart):
    count = lax.axis_size(axis)
    pairs = [[i, i ^ 1 << apart] for i in range(count) if not i >> apart & 1]
    return lax.all_gather(values, axis, axis_index_groups=pairs)


def four_exchange(copies, axis, apart):
    groups = []
    for base in range(lax.axis_size(axis)):
        if not base >> apart & 3:
            groups.append([base | g << apart for g in range(4)])
    return lax.all_to_all(copies, axis, 0, 0, axis_index_groups=groups)


def swapped(values, axis, phase):
    count_x, count_y = lax.axis_size("bx"), lax.axis_size("by")
    moves = []
    for x in range(0, count_x, 2):
        for y in range(count_y):
            place, count = (x // 2, count_x // 2) if axis == "bx" else (y, count_y)
            other = place + (1 if place % 2 == phase else -1)
            if 0 <= other < count:
                target = 2 * other * count_y + y if axis == "bx" else x * count_y + other
                moves.append((x * count_y + y, target))
    return lax.ppermute(values, BOTH, moves)


def fetched_from(values, apart):
    count_x, count_y = lax.axis_size("bx"), lax.axis_size("by")
    at = [x * count_y + y for x in range(0, count_x, 2) for y in range(count_y)]
    return lax.ppermute(values, BOTH, [(i, i ^ 1 << apart) for i in at])


def surroundings(boxes, meanwhile):
    even = lax.axis_index("bx") >> 1 & 1 == 0
    second = swapped(jnp.where(even, boxes[0], boxes[1]), "bx", 1)
    first = swapped(jnp.where(even, boxes[1], boxes[0]), "bx", 0)
    before, after = jnp.where(even, second, first), jnp.where(even, first, second)
    row = jnp.concatenate([before[None], boxes, after[None]])
    even = lax.axis_index("by") & 1 == 0
    first = swapped(row, "by", 0)
    row, meanwhile = lax.optimization_barrier((row, meanwhile))
    second = swapped(row, "by", 1)
    return jnp.where(even, second, first), row, jnp.where(even, first, second), meanwhile


class Packing:
    def __init__(self, levels, rank, excite, unknowns):
        self.excite, self.blocks = excite, unknowns // LANES
        self.split = levels - 3
        self.level_rows = 2 * rank
        self.box_rows = self.blocks * excite
        self.coeffs = self.split * self.level_rows
        self.sources = self.coeffs + excite
        self.first_rows = self.sources + self.box_rows
        self.late_rows = (levels - self.split) * self.level_rows
        self.late = 7 * self.box_rows
        self.fetched = self.late + self.late_rows
        self.second_rows = self.fetched + 2 * self.level_rows

    def place_of(self, level):
        return (level if level < self.split else level - self.split) * self.level_rows


def pack(packing, mixing_hbm, sources_hbm, project_hbm, packed, later, sources, project, sems):
    excite = packing.excite
    wide = [
        pltpu.make_async_copy(sources_hbm, sources, sems.at[0]),
        pltpu.make_async_copy(project_hbm, project, sems.at[1]),
    ]
    for copy in wide:
        copy.start()
    rest = [
        pltpu.make_async_copy(
            mixing_hbm.at[pl.ds(0, packing.coeffs)],
            packed.at[pl.ds(0, packing.coeffs)],
            sems.at[2],
        ),
        pltpu.make_async_copy(
            mixing_hbm.at[pl.ds(packing.coeffs, packing.late_rows)], later, sems.at[3]
        ),
    ]
    for block in range(packing.blocks):
        rest.append(
            pltpu.make_async_copy(
                sources_hbm.at[:, pl.ds(block * LANES, LANES)],
                packed.at[pl.ds(packing.sources + block * excite, excite)],
                sems.at[4 + block],
            )
        )
    for copy in rest:
        copy.start()
    for copy in wide:
        copy.wait()
    packed[pl.ds(packing.coeffs, excite)] = jnp.dot(
        sources[...], project[...], preferred_element_type=jnp.float32
    ).astype(jnp.bfloat16)
    for copy in rest:
        copy.wait()


def packed_own(packing, mixing, sources, project):
    vmem = pl.BlockSpec(memory_space=pltpu.VMEM)
    operands = (mixing.reshape(-1, LANES), sources, project)
    return pl.pallas_call(
        functools.partial(pack, packing),
        name="pack",
        compiler_params=GRANT,
        out_shape=tuple(
            pltpu.VMEM((rows, LANES), jnp.bfloat16)
            for rows in (packing.first_rows, packing.late_rows)
        ),
        in_specs=[pl.BlockSpec(memory_space=pl.ANY)] * 3,
        out_specs=(vmem, vmem),
        scratch_shapes=[
            pltpu.VMEM(sources.shape, sources.dtype),
            pltpu.VMEM(project.shape, project.dtype),
            pltpu.SemaphoreType.DMA((4 + packing.blocks,)),
        ],
    )(*(pltpu.with_memory_space_constraint(x, pltpu.HBM) for x in operands))


def first_level(packing, early, coeffs):
    given = [early[box, pl.ds(packing.coeffs, packing.excite)] for box in range(2)]
    for box in range(2):
        pair = jnp.concatenate([given[box], given[1 - box]], axis=1)
        coeffs[box] = jnp.dot(
            pair, early[box, pl.ds(0, packing.level_rows)], preferred_element_type=jnp.float32
        ).astype(coeffs.dtype)


def mixed(packing, level, place, both, blocks):
    axis, apart = place
    upper = lax.axis_index(axis) >> apart & 1
    if level < packing.split:
        blocks = [blocks[0].at[box] for box in range(2)]
        starts = [packing.place_of(level)] * 2
    else:
        starts = [packing.late + packing.place_of(level), packing.place_of(level)]
    sums = []
    for box in range(2):
        pair = jnp.concatenate([both[upper, box], both[1 - upper, box]], axis=1)
        weights = blocks[box][pl.ds(starts[box], packing.level_rows)]
        sums.append(
            jnp.dot(pair, weights, preferred_element_type=jnp.float32).astype(jnp.bfloat16)
        )
    return sums


def two_levels(packing, level, place, four, shared, theirs, own, coeffs):
    axis, apart = place
    rows = packing.level_rows
    bit, next_bit = (lax.axis_index(axis) >> apart + n & 1 for n in range(2))
    start = packing.place_of(level)

    def product(low, high, weights):
        pair = jnp.concatenate([low, high], axis=1)
        return jnp.dot(pair, weights, preferred_element_type=jnp.float32).astype(jnp.bfloat16)

    for box in range(2):
        near, far = 2 * next_bit, 2 * (1 - next_bit)
        here = product(
            four[near + bit, box], four[near + 1 - bit, box], shared[box, pl.ds(start, rows)]
        )
        there = product(
            four[far + bit, box],
            four[far + 1 - bit, box],
            theirs[pl.ds(packing.fetched + box * rows, rows)],
        )
        at = packing.place_of(level + 1)
        weights = theirs[pl.ds(packing.late + at, rows)] if box == 0 else own[pl.ds(at, rows)]
        coeffs[box] = product(here, there, weights)


def spread_level(packing, level, place, both, *rest):
    for box, value in enumerate(mixed(packing, level, place, both, rest[:1])):
        for member in range(4):
            rest[1][member, box] = value


def next_level(packing, level, place, both, *rest):
    blocks = rest[: 1 if level < packing.split else 2]
    coeffs = rest[len(blocks)]
    for box, value in enumerate(mixed(packing, level, place, both, blocks)):
        coeffs[box] = value


def last_level(packing, level, place, both, theirs, own, given, final):
    given[...], final[...] = mixed(packing, level, place, both, (theirs, own))


def in_vmem(kernel, out_shape, operands):
    vmem = pl.BlockSpec(memory_space=pltpu.VMEM)
    call = pl.pallas_call(
        kernel,
        compiler_params=GRANT,
        out_shape=out_shape,
        in_specs=[vmem] * len(operands),
        out_specs=jax.tree.map(lambda _: vmem, out_shape),
    )
    return call(*(pltpu.with_memory_space_constraint(x, pltpu.VMEM) for x in operands))


def near_field(
    packing, offset, beside, shared, *rest
):
    column, (near_blocks, index_ref, near, index, sem) = rest[:-5], rest[-5:]
    excite, rows = packing.excite, packing.box_rows
    targets, positions = index.shape
    block_len = near_blocks.shape[1]
    indices = pltpu.make_async_copy(index_ref, index, sem)
    indices.start()
    indices.wait()

    def block_at(x, y, block):
        at = pl.multiple_of(block * excite, excite)
        if x == 0:
            return column[0][pl.ds(y * rows + at, excite)]
        if y == 1 and x < 3:
            return shared[x - 1, pl.ds(packing.sources + at, excite)]
        return beside[pl.ds((3 if y == 1 else x - 1 + 2 * y) * rows + at, excite)]

    for target in range(targets):
        picked, blocks = [], []
        for position in range(positions):
            x, y = position // 3 + offset, position % 3
            picked.append(block_at(x, y, index[target, position]))
            start = (target * positions + position) * block_len
            blocks.append(near_blocks[pl.ds(start, block_len)])
        near[:, pl.ds(target * block_len, block_len)] = lax.dot_general(
            jnp.concatenate(picked, axis=1),
            jnp.concatenate(blocks, axis=1),
            (((1,), (1,)), ((), ())),
            preferred_element_type=jnp.float32,
        )


def near_of(packing, offset, beside, shared, column, near_blocks, near_index):
    vmem = pl.BlockSpec(memory_space=pltpu.VMEM)
    around = (beside, shared, *column)
    operands = [pltpu.with_memory_space_constraint(x, pltpu.VMEM) for x in around]
    operands += [near_blocks.reshape(-1, near_blocks.shape[3]), near_index]
    return pl.pallas_call(
        functools.partial(near_field, packing, offset),
        compiler_params=GRANT,
        out_shape=pltpu.VMEM((packing.excite, packing.blocks * LANES), jnp.float32),
        in_specs=[vmem] * len(operands),
        out_specs=vmem,
        scratch_shapes=[
            pltpu.SMEM(near_index.shape, near_index.dtype),
            pltpu.SemaphoreType.DMA,
        ],
    )(*operands)


def respond(taken, own_final, near, far_expand, response_hbm, response, sems):
    first_of_pair = lax.axis_index("bx") & 1 == 0
    final = jnp.where(first_of_pair, taken[1], own_final[...])
    width = response.shape[3] // sems.shape[0]
    copies = []
    for part in range(sems.shape[0]):
        lanes = pl.ds(part * width, width)
        response[:, 0, 0, lanes] = near[:, lanes] + jnp.dot(
            final, far_expand[:, lanes], preferred_element_type=jnp.float32
        )
        ends = response.at[:, :, :, lanes], response_hbm.at[:, :, :, lanes]
        copies.append(pltpu.make_async_copy(*ends, sems.at[part]))
        copies[-1].start()
    for copy in copies:
        copy.wait()


def response_of(taken, final, near, far_expand):
    vmem = pl.BlockSpec(memory_space=pltpu.VMEM)
    shape = (near.shape[0], 1, 1, near.shape[1])
    held = [pltpu.with_memory_space_constraint(x, pltpu.VMEM) for x in (taken, final, near)]
    return pl.pallas_call(
        respond,
        name="respond",
        compiler_params=GRANT,
        out_shape=jax.ShapeDtypeStruct(shape, jnp.float32),
        in_specs=[vmem] * 4,
        out_specs=pl.BlockSpec(memory_space=pl.ANY),
        scratch_shapes=[pltpu.VMEM(shape, jnp.float32), pltpu.SemaphoreType.DMA((4,))],
    )(*held, far_expand)


def per_device(sources, near_blocks, near_index, far_project, far_mixing, far_expand):
    own_sources, own_blocks, own_index = sources[:, 0, 0], near_blocks[0, 0], near_index[0, 0]
    excite, unknowns = own_sources.shape
    rank = far_project.shape[3]
    first_of_pair = lax.axis_index("bx") & 1 == 0
    levels = [("bx", n) for n in range(lax.axis_size("bx").bit_length() - 1)]
    levels += [("by", n) for n in range(lax.axis_size("by").bit_length() - 1)]
    packing = Packing(len(levels), rank, excite, unknowns)
    packed, later = packed_own(packing, far_mixing[0, 0], own_sources, far_project[0, 0])
    shared = pair_gather(packed, "bx", 0)
    coeffs_shape = pltpu.VMEM((2, excite, rank), jnp.bfloat16)
    four_shape = pltpu.VMEM((4, 2, excite, rank), jnp.bfloat16)
    column_shape = pltpu.VMEM((3 * packing.box_rows, LANES), jnp.bfloat16)
    given_shape = pltpu.VMEM((packing.second_rows, LANES), jnp.bfloat16)
    merged = packing.split - 1
    apart = levels[merged][1]

    def gathering():
        start = packing.place_of(merged)
        fetched = fetched_from(shared[:, start : start + packing.level_rows], apart + 1)
        boxes = shared[:, packing.sources :].reshape(2, packing.blocks, excite, LANES)
        below, row, above, fetched = surroundings(boxes, fetched)
        given = jnp.concatenate([below[1:], row[3:], above[1:]]).reshape(-1, LANES)
        column = jnp.stack([below[0], row[0], above[0]]).reshape(-1, LANES)
        given = jnp.concatenate([given, later, fetched.reshape(-1, LANES)])
        return jnp.zeros((4, 2, excite, rank), jnp.bfloat16), given, column

    def levels_early():
        coeffs = in_vmem(functools.partial(first_level, packing), coeffs_shape, (shared,))
        for level in range(1, merged):
            kernel, shape = next_level, coeffs_shape
            if level == merged - 1:
                kernel, shape = spread_level, (four_shape, given_shape, column_shape)
            both = pair_gather(coeffs, *levels[level])
            kernel = functools.partial(kernel, packing, level, levels[level])
            coeffs = in_vmem(kernel, shape, (both, shared))
        return tuple(coeffs)

    copies, given, column = lax.cond(first_of_pair, gathering, levels_early)
    handed = lax.ppermute(given, "bx", [(i, i ^ 1) for i in range(0, lax.axis_size("bx"), 2)])
    four = lax.cond(
        first_of_pair, lambda: copies, lambda: four_exchange(copies, *levels[merged])
    )

    def near_only():
        near = near_of(packing, 0, given, shared, (column,), own_blocks, own_index)
        return near, copies[0, 0], copies[0, 1]

    def levels_late():
        kernel = functools.partial(two_levels, packing, merged, levels[merged])
        result = in_vmem(kernel, coeffs_shape, (four, shared, handed, later))
        for level in range(merged + 2, len(levels)):
            kernel = functools.partial(next_level, packing, level, levels[level])
            shape = coeffs_shape
            if level == len(levels) - 1:
                kernel = functools.partial(last_level, packing, level, levels[level])
                shape = (pltpu.VMEM((excite, rank), jnp.bfloat16),) * 2
            both = pair_gather(result, *levels[level])
            result = in_vmem(kernel, shape, (both, handed, later))
        beside, result = lax.optimization_barrier((handed, tuple(result)))
        near = near_of(packing, 1, beside, shared, (), own_blocks, own_index)
        return near, *result

    near, final_given, final = lax.cond(first_of_pair, near_only, levels_late)
    taken = pair_gather(final_given, "bx", 0)
    return response_of(taken, final, near, far_expand[0, 0])


def solution(mesh):
    placed = (
        P(None, "bx", "by", None),
        P("bx", "by", None, None, None, None),
        P("bx", "by", None, None),
        P("bx", "by", None, None),
        P("bx", "by", None, None, None, None),
        P("bx", "by", None, None),
    )
    return jax.shard_map(
        per_device, mesh=mesh, in_specs=placed, out_specs=P(None, "bx", "by", None), check_vma=False
    )
```

```python
import functools

import jax
import jax.numpy as jnp
from jax import lax
from jax.experimental import pallas as pl
from jax.experimental.pallas import tpu as pltpu
from jax.sharding import PartitionSpec as P

BOTH = ("bx", "by")
LANES = 128
GRANT = pltpu.CompilerParams(vmem_limit_bytes=8 << 20)


def pair_gather(values, axis, apart):
    count = lax.axis_size(axis)
    pairs = [[i, i ^ 1 << apart] for i in range(count) if not i >> apart & 1]
    return lax.all_gather(values, axis, axis_index_groups=pairs)


def partners_of(values, apart):
    count_x, count_y = lax.axis_size("bx"), lax.axis_size("by")
    at = [x * count_y + y for x in range(1, count_x, 2) for y in range(count_y)]
    return lax.ppermute(values, BOTH, [(i, i ^ 1 << apart) for i in at])


def swapped(values, axis, phase):
    count_x, count_y = lax.axis_size("bx"), lax.axis_size("by")
    moves = []
    for x in range(0, count_x, 2):
        for y in range(count_y):
            place, count = (x // 2, count_x // 2) if axis == "bx" else (y, count_y)
            other = place + (1 if place % 2 == phase else -1)
            if 0 <= other < count:
                target = 2 * other * count_y + y if axis == "bx" else x * count_y + other
                moves.append((x * count_y + y, target))
    return lax.ppermute(values, BOTH, moves)


def surroundings(boxes):
    even = lax.axis_index("bx") >> 1 & 1 == 0
    first = swapped(jnp.where(even, boxes[1], boxes[0]), "bx", 0)
    second = swapped(jnp.where(even, boxes[0], boxes[1]), "bx", 1)
    before, after = jnp.where(even, second, first), jnp.where(even, first, second)
    row = jnp.concatenate([before[None], boxes, after[None]])
    even = lax.axis_index("by") & 1 == 0
    first, second = swapped(row, "by", 0), swapped(row, "by", 1)
    return jnp.where(even, second, first), row, jnp.where(even, first, second)


class Packing:
    def __init__(self, levels, rank, excite, unknowns):
        self.excite, self.blocks = excite, unknowns // LANES
        self.split = levels - 3
        self.level_rows = 2 * rank
        self.box_rows = self.blocks * excite
        self.coeffs = self.split * self.level_rows
        self.sources = self.coeffs + excite
        self.first_rows = self.sources + self.box_rows
        self.late_rows = (levels - self.split) * self.level_rows
        self.late = 7 * self.box_rows
        self.second_rows = self.late + self.late_rows

    def place_of(self, level):
        return (level if level < self.split else level - self.split) * self.level_rows


def pack(packing, mixing_hbm, sources_hbm, project_hbm, packed, later, sources, project, sems):
    excite = packing.excite
    wide = [
        pltpu.make_async_copy(sources_hbm, sources, sems.at[0]),
        pltpu.make_async_copy(project_hbm, project, sems.at[1]),
    ]
    for copy in wide:
        copy.start()
    rest = [
        pltpu.make_async_copy(
            mixing_hbm.at[pl.ds(0, packing.coeffs)],
            packed.at[pl.ds(0, packing.coeffs)],
            sems.at[2],
        ),
        pltpu.make_async_copy(
            mixing_hbm.at[pl.ds(packing.coeffs, packing.late_rows)], later, sems.at[3]
        ),
    ]
    for block in range(packing.blocks):
        rest.append(
            pltpu.make_async_copy(
                sources_hbm.at[:, pl.ds(block * LANES, LANES)],
                packed.at[pl.ds(packing.sources + block * excite, excite)],
                sems.at[4 + block],
            )
        )
    for copy in rest:
        copy.start()
    for copy in wide:
        copy.wait()
    packed[pl.ds(packing.coeffs, excite)] = jnp.dot(
        sources[...], project[...], preferred_element_type=jnp.float32
    ).astype(jnp.bfloat16)
    for copy in rest:
        copy.wait()


def packed_own(packing, mixing, sources, project):
    vmem = pl.BlockSpec(memory_space=pltpu.VMEM)
    operands = (mixing.reshape(-1, LANES), sources, project)
    return pl.pallas_call(
        functools.partial(pack, packing),
        name="pack",
        compiler_params=GRANT,
        out_shape=tuple(
            pltpu.VMEM((rows, LANES), jnp.bfloat16)
            for rows in (packing.first_rows, packing.late_rows)
        ),
        in_specs=[pl.BlockSpec(memory_space=pl.ANY)] * 3,
        out_specs=(vmem, vmem),
        scratch_shapes=[
            pltpu.VMEM(sources.shape, sources.dtype),
            pltpu.VMEM(project.shape, project.dtype),
            pltpu.SemaphoreType.DMA((4 + packing.blocks,)),
        ],
    )(*(pltpu.with_memory_space_constraint(x, pltpu.HBM) for x in operands))


def first_level(packing, early, coeffs):
    given = [early[box, pl.ds(packing.coeffs, packing.excite)] for box in range(2)]
    for box in range(2):
        pair = jnp.concatenate([given[box], given[1 - box]], axis=1)
        coeffs[box] = jnp.dot(
            pair, early[box, pl.ds(0, packing.level_rows)], preferred_element_type=jnp.float32
        ).astype(coeffs.dtype)


def mixed(packing, level, place, both, blocks):
    axis, apart = place
    upper = lax.axis_index(axis) >> apart & 1
    if level < packing.split:
        blocks = [blocks[0].at[box] for box in range(2)]
        starts = [packing.place_of(level)] * 2
    else:
        starts = [packing.late + packing.place_of(level), packing.place_of(level)]
    sums = []
    for box in range(2):
        pair = jnp.concatenate([both[upper, box], both[1 - upper, box]], axis=1)
        weights = blocks[box][pl.ds(starts[box], packing.level_rows)]
        sums.append(
            jnp.dot(pair, weights, preferred_element_type=jnp.float32).astype(jnp.bfloat16)
        )
    return sums


def next_level(packing, level, place, both, *rest):
    blocks = rest[: 1 if level < packing.split else 2]
    coeffs = rest[len(blocks)]
    for box, value in enumerate(mixed(packing, level, place, both, blocks)):
        coeffs[box] = value


def last_level(packing, level, place, coeffs, others, theirs, own, given, final):
    starts = [packing.late + packing.place_of(level), packing.place_of(level)]
    for box, (ref, out) in enumerate(((theirs, given), (own, final))):
        pair = jnp.concatenate([coeffs[box], others[box]], axis=1)
        weights = ref[pl.ds(starts[box], packing.level_rows)]
        out[...] = jnp.dot(pair, weights, preferred_element_type=jnp.float32).astype(out.dtype)


def in_vmem(kernel, name, out_shape, operands):
    vmem = pl.BlockSpec(memory_space=pltpu.VMEM)
    call = pl.pallas_call(
        kernel,
        name=name,
        compiler_params=GRANT,
        out_shape=out_shape,
        in_specs=[vmem] * len(operands),
        out_specs=jax.tree.map(lambda _: vmem, out_shape),
    )
    return call(*(pltpu.with_memory_space_constraint(x, pltpu.VMEM) for x in operands))


def near_field(
    packing, offset, beside, shared, *rest
):
    column, (near_blocks, index_ref, near, index, sem) = rest[:-5], rest[-5:]
    excite, rows = packing.excite, packing.box_rows
    targets, positions = index.shape
    block_len = near_blocks.shape[1]
    indices = pltpu.make_async_copy(index_ref, index, sem)
    indices.start()
    indices.wait()

    def block_at(x, y, block):
        at = pl.multiple_of(block * excite, excite)
        if x == 0:
            return column[0][pl.ds(y * rows + at, excite)]
        if y == 1 and x < 3:
            return shared[x - 1, pl.ds(packing.sources + at, excite)]
        return beside[pl.ds((3 if y == 1 else x - 1 + 2 * y) * rows + at, excite)]

    for target in range(targets):
        picked, blocks = [], []
        for position in range(positions):
            x, y = position // 3 + offset, position % 3
            picked.append(block_at(x, y, index[target, position]))
            start = (target * positions + position) * block_len
            blocks.append(near_blocks[pl.ds(start, block_len)])
        near[:, pl.ds(target * block_len, block_len)] = lax.dot_general(
            jnp.concatenate(picked, axis=1),
            jnp.concatenate(blocks, axis=1),
            (((1,), (1,)), ((), ())),
            preferred_element_type=jnp.float32,
        )


def near_of(packing, offset, beside, shared, column, near_blocks, near_index):
    vmem = pl.BlockSpec(memory_space=pltpu.VMEM)
    around = (beside, shared, *column)
    operands = [pltpu.with_memory_space_constraint(x, pltpu.VMEM) for x in around]
    operands += [near_blocks.reshape(-1, near_blocks.shape[3]), near_index]
    return pl.pallas_call(
        functools.partial(near_field, packing, offset),
        name=f"near_{offset}",
        compiler_params=GRANT,
        out_shape=pltpu.VMEM((packing.excite, packing.blocks * LANES), jnp.float32),
        in_specs=[vmem] * len(operands),
        out_specs=vmem,
        scratch_shapes=[
            pltpu.SMEM(near_index.shape, near_index.dtype),
            pltpu.SemaphoreType.DMA,
        ],
    )(*operands)


def respond(taken, own_final, near, far_expand, response_hbm, response, sems):
    first_of_pair = lax.axis_index("bx") & 1 == 0
    final = jnp.where(first_of_pair, taken[1], own_final[...])
    width = response.shape[3] // sems.shape[0]
    copies = []
    for part in range(sems.shape[0]):
        lanes = pl.ds(part * width, width)
        response[:, 0, 0, lanes] = near[:, lanes] + jnp.dot(
            final, far_expand[:, lanes], preferred_element_type=jnp.float32
        )
        ends = response.at[:, :, :, lanes], response_hbm.at[:, :, :, lanes]
        copies.append(pltpu.make_async_copy(*ends, sems.at[part]))
        copies[-1].start()
    for copy in copies:
        copy.wait()


def response_of(taken, final, near, far_expand):
    vmem = pl.BlockSpec(memory_space=pltpu.VMEM)
    shape = (near.shape[0], 1, 1, near.shape[1])
    held = [pltpu.with_memory_space_constraint(x, pltpu.VMEM) for x in (taken, final, near)]
    return pl.pallas_call(
        respond,
        name="respond",
        compiler_params=GRANT,
        out_shape=jax.ShapeDtypeStruct(shape, jnp.float32),
        in_specs=[vmem] * 4,
        out_specs=pl.BlockSpec(memory_space=pl.ANY),
        scratch_shapes=[pltpu.VMEM(shape, jnp.float32), pltpu.SemaphoreType.DMA((4,))],
    )(*held, far_expand)


def per_device(sources, near_blocks, near_index, far_project, far_mixing, far_expand):
    own_sources, own_blocks, own_index = sources[:, 0, 0], near_blocks[0, 0], near_index[0, 0]
    excite, unknowns = own_sources.shape
    rank = far_project.shape[3]
    first_of_pair = lax.axis_index("bx") & 1 == 0
    levels = [("bx", n) for n in range(lax.axis_size("bx").bit_length() - 1)]
    levels += [("by", n) for n in range(lax.axis_size("by").bit_length() - 1)]
    packing = Packing(len(levels), rank, excite, unknowns)
    packed, later = packed_own(packing, far_mixing[0, 0], own_sources, far_project[0, 0])
    shared = pair_gather(packed, "bx", 0)
    coeffs_shape = pltpu.VMEM((2, excite, rank), jnp.bfloat16)
    column_shape = pltpu.VMEM((3 * packing.box_rows, LANES), jnp.bfloat16)
    given_shape = pltpu.VMEM((packing.second_rows, LANES), jnp.bfloat16)

    def gathering():
        boxes = shared[:, packing.sources :].reshape(2, packing.blocks, excite, LANES)
        below, row, above = surroundings(boxes)
        given = jnp.concatenate([below[1:], row[3:], above[1:]]).reshape(-1, LANES)
        column = jnp.stack([below[0], row[0], above[0]]).reshape(-1, LANES)
        return jnp.zeros((2, excite, rank), jnp.bfloat16), jnp.concatenate([given, later]), column

    def levels_early():
        coeffs = in_vmem(functools.partial(first_level, packing), "level_0", coeffs_shape, (shared,))
        for level in range(1, packing.split):
            shape = coeffs_shape
            if level == packing.split - 1:
                shape = (coeffs_shape, given_shape, column_shape)
            both = pair_gather(coeffs, *levels[level])
            kernel = functools.partial(next_level, packing, level, levels[level])
            coeffs = in_vmem(kernel, f"level_{level}", shape, (both, shared))
        return tuple(coeffs)

    coeffs, given, column = lax.cond(first_of_pair, gathering, levels_early)
    handed = lax.ppermute(given, "bx", [(i, i ^ 1) for i in range(0, lax.axis_size("bx"), 2)])
    both = lax.cond(
        first_of_pair,
        lambda: jnp.stack([coeffs, coeffs]),
        lambda: pair_gather(coeffs, *levels[packing.split]),
    )

    def near_only():
        near = near_of(packing, 0, given, shared, (column,), own_blocks, own_index)
        return near, coeffs[0], coeffs[1]

    def levels_late():
        gathered, last = both, len(levels) - 1
        for level in range(packing.split, last):
            kernel = functools.partial(next_level, packing, level, levels[level])
            result = in_vmem(kernel, f"level_{level}", coeffs_shape, (gathered, handed, later))
            if level < last - 1:
                gathered = pair_gather(result, *levels[level + 1])
        others = partners_of(result, levels[last][1])
        beside, result = lax.optimization_barrier((handed, result))
        near = near_of(packing, 1, beside, shared, (), own_blocks, own_index)
        near, others = lax.optimization_barrier((near, others))
        kernel = functools.partial(last_level, packing, last, levels[last])
        shape = (pltpu.VMEM((excite, rank), jnp.bfloat16),) * 2
        return near, *in_vmem(kernel, f"level_{last}", shape, (result, others, handed, later))

    near, final_given, final = lax.cond(first_of_pair, near_only, levels_late)
    taken = pair_gather(final_given, "bx", 0)
    return response_of(taken, final, near, far_expand[0, 0])


def solution(mesh):
    placed = (
        P(None, "bx", "by", None),
        P("bx", "by", None, None, None, None),
        P("bx", "by", None, None),
        P("bx", "by", None, None),
        P("bx", "by", None, None, None, None),
        P("bx", "by", None, None),
    )
    return jax.shard_map(
        per_device, mesh=mesh, in_specs=placed, out_specs=P(None, "bx", "by", None), check_vma=False
    )
```

```python
import functools

import jax
import jax.numpy as jnp
from jax import lax
from jax.experimental import pallas as pl
from jax.experimental.pallas import tpu as pltpu
from jax.sharding import PartitionSpec as P

BOTH = ("bx", "by")
LANES = 128
GRANT = pltpu.CompilerParams(vmem_limit_bytes=8 << 20)


def pair_gather(values, axis, apart):
    count = lax.axis_size(axis)
    pairs = [[i, i ^ 1 << apart] for i in range(count) if not i >> apart & 1]
    return lax.all_gather(values, axis, axis_index_groups=pairs)


def partners_of(values, apart):
    count_x, count_y = lax.axis_size("bx"), lax.axis_size("by")
    at = [x * count_y + y for x in range(1, count_x, 2) for y in range(count_y)]
    return lax.ppermute(values, BOTH, [(i, i ^ 1 << apart) for i in at])


def swapped(values, axis, phase):
    count_x, count_y = lax.axis_size("bx"), lax.axis_size("by")
    moves = []
    for x in range(0, count_x, 2):
        for y in range(count_y):
            place, count = (x // 2, count_x // 2) if axis == "bx" else (y, count_y)
            other = place + (1 if place % 2 == phase else -1)
            if 0 <= other < count:
                target = 2 * other * count_y + y if axis == "bx" else x * count_y + other
                moves.append((x * count_y + y, target))
    return lax.ppermute(values, BOTH, moves)


def surroundings(boxes):
    even = lax.axis_index("bx") >> 1 & 1 == 0
    first = swapped(jnp.where(even, boxes[1], boxes[0]), "bx", 0)
    second = swapped(jnp.where(even, boxes[0], boxes[1]), "bx", 1)
    before, after = jnp.where(even, second, first), jnp.where(even, first, second)
    row = jnp.concatenate([before[None], boxes, after[None]])
    even = lax.axis_index("by") & 1 == 0
    first, second = swapped(row, "by", 0), swapped(row, "by", 1)
    return jnp.where(even, second, first), row, jnp.where(even, first, second)


class Packing:
    def __init__(self, levels, rank, excite, unknowns):
        self.excite, self.blocks = excite, unknowns // LANES
        self.split = levels - 3
        self.level_rows = 2 * rank
        self.box_rows = self.blocks * excite
        self.coeffs = self.split * self.level_rows
        self.sources = self.coeffs + excite
        self.first_rows = self.sources + self.box_rows
        self.late_rows = (levels - self.split) * self.level_rows
        self.late = 7 * self.box_rows
        self.second_rows = self.late + self.late_rows

    def place_of(self, level):
        return (level if level < self.split else level - self.split) * self.level_rows


def pack(packing, mixing_hbm, sources_hbm, project_hbm, packed, later, sources, project, sems):
    excite = packing.excite
    wide = [
        pltpu.make_async_copy(sources_hbm, sources, sems.at[0]),
        pltpu.make_async_copy(project_hbm, project, sems.at[1]),
    ]
    for copy in wide:
        copy.start()
    rest = [
        pltpu.make_async_copy(
            mixing_hbm.at[pl.ds(0, packing.coeffs)],
            packed.at[pl.ds(0, packing.coeffs)],
            sems.at[2],
        ),
        pltpu.make_async_copy(
            mixing_hbm.at[pl.ds(packing.coeffs, packing.late_rows)], later, sems.at[3]
        ),
    ]
    for block in range(packing.blocks):
        rest.append(
            pltpu.make_async_copy(
                sources_hbm.at[:, pl.ds(block * LANES, LANES)],
                packed.at[pl.ds(packing.sources + block * excite, excite)],
                sems.at[4 + block],
            )
        )
    for copy in rest:
        copy.start()
    for copy in wide:
        copy.wait()
    packed[pl.ds(packing.coeffs, excite)] = jnp.dot(
        sources[...], project[...], preferred_element_type=jnp.float32
    ).astype(jnp.bfloat16)
    for copy in rest:
        copy.wait()


def packed_own(packing, mixing, sources, project):
    vmem = pl.BlockSpec(memory_space=pltpu.VMEM)
    operands = (mixing.reshape(-1, LANES), sources, project)
    return pl.pallas_call(
        functools.partial(pack, packing),
        name="pack",
        compiler_params=GRANT,
        out_shape=tuple(
            pltpu.VMEM((rows, LANES), jnp.bfloat16)
            for rows in (packing.first_rows, packing.late_rows)
        ),
        in_specs=[pl.BlockSpec(memory_space=pl.ANY)] * 3,
        out_specs=(vmem, vmem),
        scratch_shapes=[
            pltpu.VMEM(sources.shape, sources.dtype),
            pltpu.VMEM(project.shape, project.dtype),
            pltpu.SemaphoreType.DMA((4 + packing.blocks,)),
        ],
    )(*(pltpu.with_memory_space_constraint(x, pltpu.HBM) for x in operands))


def first_level(packing, early, coeffs):
    given = [early[box, pl.ds(packing.coeffs, packing.excite)] for box in range(2)]
    for box in range(2):
        pair = jnp.concatenate([given[box], given[1 - box]], axis=1)
        coeffs[box] = jnp.dot(
            pair, early[box, pl.ds(0, packing.level_rows)], preferred_element_type=jnp.float32
        ).astype(coeffs.dtype)


def mixed(packing, level, place, both, blocks):
    axis, apart = place
    upper = lax.axis_index(axis) >> apart & 1
    if level < packing.split:
        blocks = [blocks[0].at[box] for box in range(2)]
        starts = [packing.place_of(level)] * 2
    else:
        starts = [packing.late + packing.place_of(level), packing.place_of(level)]
    sums = []
    for box in range(2):
        pair = jnp.concatenate([both[upper, box], both[1 - upper, box]], axis=1)
        weights = blocks[box][pl.ds(starts[box], packing.level_rows)]
        sums.append(
            jnp.dot(pair, weights, preferred_element_type=jnp.float32).astype(jnp.bfloat16)
        )
    return sums


def next_level(packing, level, place, both, *rest):
    blocks = rest[: 1 if level < packing.split else 2]
    coeffs = rest[len(blocks)]
    for box, value in enumerate(mixed(packing, level, place, both, blocks)):
        coeffs[box] = value


def last_level(packing, level, place, coeffs, others, theirs, own, given, final):
    starts = [packing.late + packing.place_of(level), packing.place_of(level)]
    for box, (ref, out) in enumerate(((theirs, given), (own, final))):
        pair = jnp.concatenate([coeffs[box], others[box]], axis=1)
        weights = ref[pl.ds(starts[box], packing.level_rows)]
        out[...] = jnp.dot(pair, weights, preferred_element_type=jnp.float32).astype(out.dtype)


def in_vmem(kernel, name, out_shape, operands):
    vmem = pl.BlockSpec(memory_space=pltpu.VMEM)
    call = pl.pallas_call(
        kernel,
        name=name,
        compiler_params=GRANT,
        cost_estimate=pl.CostEstimate(
            flops=4 * 10**9, bytes_accessed=16 << 20, transcendentals=0
        ),
        out_shape=out_shape,
        in_specs=[vmem] * len(operands),
        out_specs=jax.tree.map(lambda _: vmem, out_shape),
    )
    return call(*(pltpu.with_memory_space_constraint(x, pltpu.VMEM) for x in operands))


def near_field(
    packing, offset, beside, shared, *rest
):
    column, (near_blocks, index_ref, near, index, sem) = rest[:-5], rest[-5:]
    excite, rows = packing.excite, packing.box_rows
    targets, positions = index.shape
    block_len = near_blocks.shape[1]
    indices = pltpu.make_async_copy(index_ref, index, sem)
    indices.start()
    indices.wait()

    def block_at(x, y, block):
        at = pl.multiple_of(block * excite, excite)
        if x == 0:
            return column[0][pl.ds(y * rows + at, excite)]
        if y == 1 and x < 3:
            return shared[x - 1, pl.ds(packing.sources + at, excite)]
        return beside[pl.ds((3 if y == 1 else x - 1 + 2 * y) * rows + at, excite)]

    for target in range(targets):
        picked, blocks = [], []
        for position in range(positions):
            x, y = position // 3 + offset, position % 3
            picked.append(block_at(x, y, index[target, position]))
            start = (target * positions + position) * block_len
            blocks.append(near_blocks[pl.ds(start, block_len)])
        near[:, pl.ds(target * block_len, block_len)] = lax.dot_general(
            jnp.concatenate(picked, axis=1),
            jnp.concatenate(blocks, axis=1),
            (((1,), (1,)), ((), ())),
            preferred_element_type=jnp.float32,
        )


def near_of(packing, offset, beside, shared, column, near_blocks, near_index):
    vmem = pl.BlockSpec(memory_space=pltpu.VMEM)
    around = (beside, shared, *column)
    operands = [pltpu.with_memory_space_constraint(x, pltpu.VMEM) for x in around]
    operands += [near_blocks.reshape(-1, near_blocks.shape[3]), near_index]
    return pl.pallas_call(
        functools.partial(near_field, packing, offset),
        name=f"near_{offset}",
        compiler_params=GRANT,
        out_shape=pltpu.VMEM((packing.excite, packing.blocks * LANES), jnp.float32),
        in_specs=[vmem] * len(operands),
        out_specs=vmem,
        scratch_shapes=[
            pltpu.SMEM(near_index.shape, near_index.dtype),
            pltpu.SemaphoreType.DMA,
        ],
    )(*operands)


def respond(taken, own_final, near, far_expand, response_hbm, response, sems):
    first_of_pair = lax.axis_index("bx") & 1 == 0
    final = jnp.where(first_of_pair, taken[1], own_final[...])
    width = response.shape[3] // sems.shape[0]
    copies = []
    for part in range(sems.shape[0]):
        lanes = pl.ds(part * width, width)
        response[:, 0, 0, lanes] = near[:, lanes] + jnp.dot(
            final, far_expand[:, lanes], preferred_element_type=jnp.float32
        )
        ends = response.at[:, :, :, lanes], response_hbm.at[:, :, :, lanes]
        copies.append(pltpu.make_async_copy(*ends, sems.at[part]))
        copies[-1].start()
    for copy in copies:
        copy.wait()


def response_of(taken, final, near, far_expand):
    vmem = pl.BlockSpec(memory_space=pltpu.VMEM)
    shape = (near.shape[0], 1, 1, near.shape[1])
    held = [pltpu.with_memory_space_constraint(x, pltpu.VMEM) for x in (taken, final, near)]
    return pl.pallas_call(
        respond,
        name="respond",
        compiler_params=GRANT,
        out_shape=jax.ShapeDtypeStruct(shape, jnp.float32),
        in_specs=[vmem] * 4,
        out_specs=pl.BlockSpec(memory_space=pl.ANY),
        scratch_shapes=[pltpu.VMEM(shape, jnp.float32), pltpu.SemaphoreType.DMA((4,))],
    )(*held, far_expand)


def per_device(sources, near_blocks, near_index, far_project, far_mixing, far_expand):
    own_sources, own_blocks, own_index = sources[:, 0, 0], near_blocks[0, 0], near_index[0, 0]
    excite, unknowns = own_sources.shape
    rank = far_project.shape[3]
    first_of_pair = lax.axis_index("bx") & 1 == 0
    levels = [("bx", n) for n in range(lax.axis_size("bx").bit_length() - 1)]
    levels += [("by", n) for n in range(lax.axis_size("by").bit_length() - 1)]
    packing = Packing(len(levels), rank, excite, unknowns)
    packed, later = packed_own(packing, far_mixing[0, 0], own_sources, far_project[0, 0])
    shared = pair_gather(packed, "bx", 0)
    coeffs_shape = pltpu.VMEM((2, excite, rank), jnp.bfloat16)
    column_shape = pltpu.VMEM((3 * packing.box_rows, LANES), jnp.bfloat16)
    given_shape = pltpu.VMEM((packing.second_rows, LANES), jnp.bfloat16)

    def gathering():
        boxes = shared[:, packing.sources :].reshape(2, packing.blocks, excite, LANES)
        below, row, above = surroundings(boxes)
        given = jnp.concatenate([below[1:], row[3:], above[1:]]).reshape(-1, LANES)
        column = jnp.stack([below[0], row[0], above[0]]).reshape(-1, LANES)
        return jnp.zeros((2, excite, rank), jnp.bfloat16), jnp.concatenate([given, later]), column

    def levels_early():
        coeffs = in_vmem(functools.partial(first_level, packing), "level_0", coeffs_shape, (shared,))
        for level in range(1, packing.split):
            shape = coeffs_shape
            if level == packing.split - 1:
                shape = (coeffs_shape, given_shape, column_shape)
            both = pair_gather(coeffs, *levels[level])
            kernel = functools.partial(next_level, packing, level, levels[level])
            coeffs = in_vmem(kernel, f"level_{level}", shape, (both, shared))
        return tuple(coeffs)

    coeffs, given, column = lax.cond(first_of_pair, gathering, levels_early)
    handed = lax.ppermute(given, "bx", [(i, i ^ 1) for i in range(0, lax.axis_size("bx"), 2)])
    both = lax.cond(
        first_of_pair,
        lambda: jnp.stack([coeffs, coeffs]),
        lambda: pair_gather(coeffs, *levels[packing.split]),
    )

    def near_only():
        near = near_of(packing, 0, given, shared, (column,), own_blocks, own_index)
        return near, coeffs[0], coeffs[1]

    def levels_late():
        gathered, last = both, len(levels) - 1
        for level in range(packing.split, last):
            kernel = functools.partial(next_level, packing, level, levels[level])
            result = in_vmem(kernel, f"level_{level}", coeffs_shape, (gathered, handed, later))
            if level < last - 1:
                gathered = pair_gather(result, *levels[level + 1])
        others = partners_of(result, levels[last][1])
        beside, result = lax.optimization_barrier((handed, result))
        near = near_of(packing, 1, beside, shared, (), own_blocks, own_index)
        near, others = lax.optimization_barrier((near, others))
        kernel = functools.partial(last_level, packing, last, levels[last])
        shape = (pltpu.VMEM((excite, rank), jnp.bfloat16),) * 2
        return near, *in_vmem(kernel, f"level_{last}", shape, (result, others, handed, later))

    near, final_given, final = lax.cond(first_of_pair, near_only, levels_late)
    taken = pair_gather(final_given, "bx", 0)
    return response_of(taken, final, near, far_expand[0, 0])


def solution(mesh):
    placed = (
        P(None, "bx", "by", None),
        P("bx", "by", None, None, None, None),
        P("bx", "by", None, None),
        P("bx", "by", None, None),
        P("bx", "by", None, None, None, None),
        P("bx", "by", None, None),
    )
    return jax.shard_map(
        per_device, mesh=mesh, in_specs=placed, out_specs=P(None, "bx", "by", None), check_vma=False
    )
```
